32 devices in a mesh: sample: 2 (over x), row: 16 (over z, y, core).
Axes of the slice: x: 2, y: 2, z: 4, core: 2. Of those that a mesh axis runs over, the one named last changes fastest.
Arguments:
- sample_index: int32 [2], P('sample'), parts along dimension 0, may hold values from 0 to 32767
- lattice_vector: int32 [1024], replicated, may hold values from 1 to 32767
- mode_table: int32 [2, 1024], replicated, may hold values from -16 to 31, as said below
- connectivity: int32 [3, 32768], replicated, may hold values from 0 to 16639, as said below
- density: bfloat16 [64, 32768], P(None, 'row'), may hold values from -3.5 to 3.5
Outputs:
- potential: float32 [8192, 64], P(('sample', 'row')), parts along dimension 0
The draws below stay inside these ranges and needn't reach their ends.
There are 2 independent parts, one for each index of `sample`. The reference program is written for one: setup_inputs(seed, part) draws one part's arguments, and reference() takes and returns one part's arrays. A program takes and returns all parts, laid end to end along the dimension named above; an argument that names none is the same for every part. Nothing has to cross between parts.
Inputs may be any that keep to these rules, and one draw needn't show every extreme that they name: `mode_table`: the 1024 columns are distinct frequency pairs, the polar one from 0 to 31 and the azimuthal one from -16 to 15. `connectivity`: vertex i * 256 + j lies on latitude cycle i and azimuth j. The columns are the triangles of that grid, two per cell between neighbouring cycles (azimuth wrapping around), each once and oriented with outward normals, in random order.
All inputs are finite; a program needn't handle non-finite values.
Results may differ from the reference program's by a relative error of at most 0.0035.
Values may be sent and summed in bfloat16 or wider, within the bound.
A program may use at most 256 MiB of HBM per device.

```python
import math
import jax
import jax.numpy as jnp
from jax import lax

COLS = 64
MODES = 1024
NLAT = 32768
NPH = 256
SRC_DEV = 2048
BAND_DEV = 256
PANELS = 32768
BAND = 4096
NT = 65


def quad_layout(key):
    quad_total = (NT - 1) * NPH
    canonical = jnp.arange(2 * quad_total, dtype=jnp.int32)
    shuffled = jax.random.permutation(jax.random.fold_in(key, 11), canonical)
    quad_index = shuffled // 2
    return (quad_index // NPH, quad_index % NPH, shuffled % 2)


def draw_mode_table(key, part):
    chosen = jax.random.permutation(jax.random.fold_in(key, 1), jnp.arange(1024, dtype=jnp.int32))[:MODES]
    polar_freq = chosen // 32
    azim_freq = chosen % 32 - 16
    return jnp.stack([polar_freq, azim_freq]).astype(jnp.int32)


def draw_connectivity(key, part):
    cycle_index, column_index, upper_half = quad_layout(key)
    next_column = (column_index + 1) % NPH
    vertex_aa = cycle_index * NPH + column_index
    vertex_ba = (cycle_index + 1) * NPH + column_index
    vertex_ab = cycle_index * NPH + next_column
    vertex_bb = (cycle_index + 1) * NPH + next_column
    corner_one = jnp.where(upper_half == 0, vertex_aa, vertex_ba)
    corner_two = jnp.where(upper_half == 0, vertex_ba, vertex_bb)
    return jnp.stack([corner_one, corner_two, vertex_ab]).astype(jnp.int32)


def draw_density(key, part):
    cycle_index, column_index, upper_half = quad_layout(key)
    polar_mid = math.pi * (cycle_index.astype(jnp.float32) + 1.5) / (NT + 1)
    azim_mid = 2.0 * math.pi * (column_index.astype(jnp.float32) + 0.5) / NPH
    coef_one = jax.random.uniform(jax.random.fold_in(key, 31), (COLS, 1), jnp.float32, -0.8, 0.8)
    coef_two = jax.random.uniform(jax.random.fold_in(key, 32), (COLS, 1), jnp.float32, -0.8, 0.8)
    phase = jax.random.uniform(jax.random.fold_in(key, 33), (COLS, 1), jnp.float32, -math.pi, math.pi)
    sector_count = 2 ** jax.random.randint(jax.random.fold_in(key, 34), (COLS, 1), 1, 4)
    sector_offset = jax.random.randint(jax.random.fold_in(key, 35), (COLS, 1), 0, NPH)
    sector_index = (column_index[None, :] + sector_offset) % NPH * sector_count // NPH
    sector_sign = (1 - 2 * (sector_index % 2)).astype(jnp.float32)
    smooth = 0.6 + coef_one * jnp.cos(polar_mid)[None, :] + coef_two * jnp.sin(polar_mid)[None, :] * jnp.cos(azim_mid[None, :] - phase)
    level_key = jax.random.fold_in(key, 36)
    rough_key = jax.random.fold_in(key, 37)
    levels = jax.random.uniform(level_key, (COLS, 1), jnp.float32, 0.6, 1.2)
    rough = 0.25 * jnp.clip(jax.random.normal(rough_key, (COLS, PANELS), jnp.float32), -3.0, 3.0)
    return (levels * smooth * sector_sign + rough).astype(jnp.bfloat16)


def with_ends(values, own_key, smallest, high):
    longest = values.shape.index(max(values.shape))
    spots = []
    for shift in (0, 1):
        where = [jax.random.randint(jax.random.fold_in(own_key, axis), (), 0, length) for axis, length in enumerate(values.shape)]
        where[longest] = (where[longest] + shift) % values.shape[longest]
        spots.append(tuple(where))
    return values.at[spots[0]].set(smallest).at[spots[1]].set(high)


def setup_inputs(seed: int = 0, part: int = 0) -> dict:
    key_of = jax.random.split(jax.random.key(seed), 6)
    part_keys = jax.random.split(jax.random.fold_in(key_of[5], part), 6)
    return {
        "sample_index": jax.random.randint(part_keys[0], (1,), 0, NLAT).astype(jnp.int32),
        "lattice_vector": with_ends(jax.random.randint(key_of[1], (MODES,), 1, NLAT), jax.random.fold_in(key_of[1], 1), 1, NLAT - 1).astype(jnp.int32),
        "mode_table": draw_mode_table(jax.random.fold_in(key_of[5], 71), part),
        "connectivity": draw_connectivity(jax.random.fold_in(key_of[5], 71), part),
        "density": draw_density(jax.random.fold_in(key_of[5], 71), part),
    }


def vertex_grid(sample_index, lattice_vector, mode_table, cycle_count):
    lattice_steps = sample_index[0] * lattice_vector % NLAT
    shifts = lattice_steps.astype(jnp.float32) / NLAT - 0.5
    polar_freq = mode_table[0].astype(jnp.float32)
    azim_freq = mode_table[1].astype(jnp.float32)
    mode_coef = 0.8 * shifts / (1.0 + polar_freq + jnp.abs(azim_freq)) ** 2
    polar_angle = math.pi * (jnp.arange(cycle_count, dtype=jnp.float32) + 1.0) / (cycle_count + 1)
    azimuth = 2.0 * math.pi * jnp.arange(NPH, dtype=jnp.float32) / NPH
    polar_phase = polar_angle[:, None] * polar_freq[None, :]
    azim_phase = azim_freq[:, None] * azimuth[None, :]
    cos_part = jnp.dot(jnp.cos(polar_phase) * mode_coef[None, :], jnp.cos(azim_phase), precision=lax.Precision.HIGHEST)
    sin_part = jnp.dot(jnp.sin(polar_phase) * mode_coef[None, :], jnp.sin(azim_phase), precision=lax.Precision.HIGHEST)
    radius = jnp.exp(cos_part - sin_part)
    cycle_sin = jnp.sin(polar_angle)[:, None]
    coord_x = radius * cycle_sin * jnp.cos(azimuth)[None, :]
    coord_y = radius * cycle_sin * jnp.sin(azimuth)[None, :]
    coord_z = radius * jnp.cos(polar_angle)[:, None]
    return jnp.stack([coord_x, coord_y, coord_z]).reshape(3, cycle_count * NPH)

def panel_geometry(vertices, corners):
    corner_one = vertices[:, corners[0]]
    corner_two = vertices[:, corners[1]]
    corner_three = vertices[:, corners[2]]
    centers = (corner_one + corner_two + corner_three) / 3.0
    edge_one = corner_two - corner_one
    edge_two = corner_three - corner_one
    area_vectors = 0.5 * jnp.stack([edge_one[1] * edge_two[2] - edge_one[2] * edge_two[1], edge_one[2] * edge_two[0] - edge_one[0] * edge_two[2], edge_one[0] * edge_two[1] - edge_one[1] * edge_two[0]])
    return (centers, area_vectors)

def kernel_tile(target_centers, target_ids, source_centers, source_areas, source_ids):
    delta_x = target_centers[0][:, None] - source_centers[0][None, :]
    delta_y = target_centers[1][:, None] - source_centers[1][None, :]
    delta_z = target_centers[2][:, None] - source_centers[2][None, :]
    dist_sq = delta_x * delta_x + delta_y * delta_y + delta_z * delta_z
    self_pair = target_ids[:, None] == source_ids[None, :]
    safe_dist = jnp.where(self_pair, 1.0, dist_sq)
    numerator = delta_x * source_areas[0][None, :] + delta_y * source_areas[1][None, :] + delta_z * source_areas[2][None, :]
    kernel_value = numerator / (4.0 * math.pi * safe_dist * jnp.sqrt(safe_dist))
    return jnp.where(self_pair, 0.0, kernel_value).astype(jnp.bfloat16)

def reference(sample_index, lattice_vector, mode_table, connectivity, density):
    vertices = vertex_grid(sample_index, lattice_vector, mode_table, NT)
    centers, area_vectors = panel_geometry(vertices, connectivity)
    source_ids = jnp.arange(PANELS, dtype=jnp.int32)
    band_rows = jnp.arange(BAND, dtype=jnp.int32)
    band_panel = band_rows // BAND_DEV * SRC_DEV + band_rows % BAND_DEV
    block = math.gcd(BAND, 256)

    def one_block(turn):
        first_row = turn * block
        target_ids = lax.dynamic_slice_in_dim(band_panel, first_row, block, 0)
        target_centers = centers[:, target_ids]
        tile = kernel_tile(target_centers, target_ids, centers, area_vectors, source_ids)
        return lax.dot_general(tile, density, (((1,), (1,)), ((), ())), preferred_element_type=jnp.float32)
    sums = lax.map(one_block, jnp.arange(BAND // block, dtype=jnp.int32)).reshape(BAND, COLS)
    local_term = 0.5 * density[:, band_panel].astype(jnp.float32).T
    return local_term + sums
```

```python
import functools
import math

import jax
import jax.numpy as jnp
import numpy as np
from jax import lax
from jax.experimental import pallas as pl
from jax.experimental.pallas import tpu as pltpu
from jax.sharding import PartitionSpec as P

NLAT = 32768
NPH = 256
BAND_DEV = 256
POLAR = 32
AZIM = 32
AZIM_LOW = -16
NUMER = 21
KDIM = 64
CHUNK = 256
SRC_TILE = 256
SQUARED = 176

F32 = jnp.float32
BF16 = jnp.bfloat16


def round_up(value, step):
    return -(-value // step) * step


def split3(value):
    high = value.astype(BF16)
    rest = value - high.astype(F32)
    mid = rest.astype(BF16)
    low = (rest - mid.astype(F32)).astype(BF16)
    return high, mid, low


def split3_np(value):
    import ml_dtypes

    value = value.astype(np.float32)
    high = value.astype(ml_dtypes.bfloat16)
    rest = value - high.astype(np.float32)
    mid = rest.astype(ml_dtypes.bfloat16)
    low = (rest - mid.astype(np.float32)).astype(ml_dtypes.bfloat16)
    return [high, mid, low]


def pair_rows(split, rest, axes, target):
    one = jnp.ones_like(rest)
    rows = []
    for axis in axes:
        high = split[axis][0]
        whole = high * high
        first = whole.astype(BF16).astype(F32)
        second = whole - first
        rows += [first, one, high, second, one] if target else [one, first, -2.0 * high, one, second]
    for part in split3(rest):
        part = part.astype(F32)
        rows += [part, one] if target else [one, part]
    for axis in axes:
        high, mid, low = split[axis]
        if target:
            rows += [high, mid, mid, high, low, mid, low]
        else:
            high, mid, low = -2.0 * high, -2.0 * mid, -2.0 * low
            rows += [mid, high, mid, low, high, low, mid]
    return rows


def split_point(center):
    split = [[part.astype(F32) for part in split3(value)] for value in center]
    rest = None
    for value, parts in zip(center, split):
        term = (value - parts[0]) * (value + parts[0])
        rest = term if rest is None else rest + term
    return split, rest


def tables(cycle_count, padded):
    angle = np.pi * (np.arange(cycle_count) + 1.0) / (cycle_count + 1)
    azimuth = 2.0 * np.pi * np.arange(NPH) / NPH
    polar = np.arange(POLAR)
    azim = np.arange(AZIM) + AZIM_LOW
    pol = np.zeros((padded, 2 * POLAR), np.float32)
    pol[:cycle_count, :POLAR] = np.cos(angle[:, None] * polar[None])
    pol[:cycle_count, POLAR:] = np.sin(angle[:, None] * polar[None])
    azi = np.concatenate(
        [np.cos(azim[:, None] * azimuth[None]), -np.sin(azim[:, None] * azimuth[None])]
    ).astype(np.float32)
    after = np.roll(azimuth, -1)
    rows = []
    for field in (np.cos(azimuth), np.sin(azimuth), np.cos(after), np.sin(after)):
        rows += split3_np(field)
    azim_rows = np.zeros((16, NPH), rows[0].dtype)
    azim_rows[:12] = np.stack(rows)
    rows = []
    full = np.zeros(padded + 1)
    for func in (np.sin, np.cos):
        full[:cycle_count] = func(angle)
        rows += split3_np(full[:-1])
    for func in (np.sin, np.cos):
        full[:cycle_count] = func(angle)
        rows += split3_np(full[1:])
    polar_rows = np.zeros((16, padded), rows[0].dtype)
    polar_rows[:12] = np.stack(rows)
    return pol, azi, azim_rows, polar_rows


def dot_hi(left, right):
    return jnp.dot(left, right, precision=lax.Precision.HIGHEST, preferred_element_type=F32)


def geometry(
    padded, src_dev, row_total, wait_conn,
    sample_ref, lattice_ref, mode_ref, conn_ref, pol_ref, azi_ref, azim_rows_ref, polar_rows_ref,
    target_k_ref, target_c_ref, source_k_ref, source_d_ref, source_b_ref,
    table_ref, rows_ref,
):
    me = lax.axis_index("row")
    side_of_pair = lax.rem(me, 2)
    steps = (sample_ref[0] * lattice_ref[...]) & (NLAT - 1)
    shifts = steps.astype(F32) / NLAT - 0.5
    polar = mode_ref[0:1, :]
    azim = mode_ref[1:2, :]
    scale = 1.0 + polar.astype(F32) + jnp.abs(azim.astype(F32))
    coef = 0.8 * shifts / (scale * scale)
    modes = coef.shape[1]
    at_polar = lax.broadcasted_iota(jnp.int32, (POLAR, modes), 0) == polar
    at_azim = lax.broadcasted_iota(jnp.int32, (AZIM, modes), 0) + AZIM_LOW == azim
    azim_hot = jnp.where(at_azim, 1.0, 0.0).astype(BF16)
    grid = jnp.zeros((POLAR, AZIM), F32)
    for part in split3(jnp.where(at_polar, coef, 0.0)):
        grid += lax.dot_general(part, azim_hot, (((1,), (1,)), ((), ())), preferred_element_type=F32)
    cos_half = dot_hi(grid, azi_ref[0:AZIM, :])
    sin_half = dot_hi(grid, azi_ref[AZIM:2 * AZIM, :])
    log_radius = dot_hi(pol_ref[:, 0:POLAR], cos_half) + dot_hi(pol_ref[:, POLAR:2 * POLAR], sin_half)
    radius = jnp.exp(log_radius)
    after = pltpu.roll(radius, NPH - 1, 1)
    for index, part in enumerate(split3(radius) + split3(after)):
        table_ref[index * padded:(index + 1) * padded, :] = part
    table_ref[6 * padded:6 * padded + 16, :] = azim_rows_ref[...]
    rows_ref[...] = jnp.zeros_like(rows_ref)
    wait_conn()

    def corners_of(corner):
        azim_all = corner & (NPH - 1)
        cycle_all = corner // NPH
        azim_k = [azim_all[k:k + 1, :] for k in range(3)]
        cycle_k = [cycle_all[k:k + 1, :] for k in range(3)]
        cycle0 = jnp.minimum(jnp.minimum(cycle_k[0], cycle_k[1]), cycle_k[2])
        low = jnp.minimum(jnp.minimum(azim_k[0], azim_k[1]), azim_k[2])
        high = jnp.maximum(jnp.maximum(azim_k[0], azim_k[1]), azim_k[2])
        azim0 = jnp.where(high - low > 1, high, low)
        hot = jnp.where(
            lax.broadcasted_iota(jnp.int32, (NPH, CHUNK), 0) == azim0, 1.0, 0.0
        ).astype(BF16)
        picked = jnp.dot(table_ref[...], hot, preferred_element_type=F32)
        near = picked[0:padded] + picked[padded:2 * padded] + picked[2 * padded:3 * padded]
        far = picked[3 * padded:4 * padded] + picked[4 * padded:5 * padded] + picked[5 * padded:6 * padded]
        tail = picked[6 * padded:6 * padded + 16]
        cycles = lax.broadcasted_iota(jnp.int32, (padded, CHUNK), 0)
        here = cycles == cycle0
        below = cycles == cycle0 + 1

        def take(mask, field):
            return jnp.sum(jnp.where(mask, field, 0.0), axis=0, keepdims=True)

        radius_of = ((take(here, near), take(here, far)), (take(below, near), take(below, far)))
        cycle_hot = jnp.where(here, 1.0, 0.0).astype(BF16)
        turn = jnp.dot(polar_rows_ref[...], cycle_hot, preferred_element_type=F32)

        def join(rows, start):
            return rows[start:start + 1] + rows[start + 1:start + 2] + rows[start + 2:start + 3]

        sin_t = (join(turn, 0), join(turn, 6))
        cos_t = (join(turn, 3), join(turn, 9))
        cos_f = (join(tail, 0), join(tail, 6))
        sin_f = (join(tail, 3), join(tail, 9))
        points = []
        for k in range(3):
            down = cycle_k[k] != cycle0
            side = azim_k[k] != azim0
            radius_k = jnp.where(
                down,
                jnp.where(side, radius_of[1][1], radius_of[1][0]),
                jnp.where(side, radius_of[0][1], radius_of[0][0]),
            )
            ring = radius_k * jnp.where(down, sin_t[1], sin_t[0])
            points.append((
                ring * jnp.where(side, cos_f[1], cos_f[0]),
                ring * jnp.where(side, sin_f[1], sin_f[0]),
                radius_k * jnp.where(down, cos_t[1], cos_t[0]),
            ))
        return points

    def center_of(points):
        return [(points[0][axis] + points[1][axis] + points[2][axis]) / 3.0 for axis in range(3)]

    def target_chunk(turn, carry):
        first = pl.multiple_of((2 * turn + side_of_pair) * src_dev, src_dev)
        center = center_of(corners_of(conn_ref[:, pl.ds(first, CHUNK)]))
        place = pl.ds(pl.multiple_of(turn * CHUNK, CHUNK), CHUNK)
        split, rest = split_point(center)
        for axis in range(3):
            target_c_ref[axis:axis + 1, place] = center[axis]
            high, mid, low = split[axis]
            for index, part in enumerate((high, high, high, mid, mid, low)):
                rows_ref[6 * axis + index:6 * axis + index + 1, :] = part
        rows_ref[18:21, :] = jnp.ones((3, CHUNK), F32)
        for index, part in enumerate(pair_rows(split, rest, (2, 0, 1), True)):
            rows_ref[NUMER + index:NUMER + index + 1, :] = part
        target_k_ref[:, place] = rows_ref[0:KDIM, :].astype(BF16)
        return carry

    def source_chunk(turn, carry):
        first = pl.multiple_of((me - side_of_pair) * src_dev + turn * CHUNK, CHUNK)
        points = corners_of(conn_ref[:, pl.ds(first, CHUNK)])
        center = center_of(points)
        one = [points[1][axis] - points[0][axis] for axis in range(3)]
        two = [points[2][axis] - points[0][axis] for axis in range(3)]
        factor = 0.5 / (4.0 * math.pi)
        area = [
            factor * (one[1] * two[2] - one[2] * two[1]),
            factor * (one[2] * two[0] - one[0] * two[2]),
            factor * (one[0] * two[1] - one[1] * two[0]),
        ]
        for axis in range(3):
            high, mid, low = [part.astype(F32) for part in split3(area[axis])]
            for index, part in enumerate((high, mid, low, high, mid, high)):
                rows_ref[6 * axis + index:6 * axis + index + 1, :] = part
        base = -(center[0] * area[0] + center[1] * area[1] + center[2] * area[2])
        for index, part in enumerate(split3(base)):
            rows_ref[18 + index:19 + index, :] = part.astype(F32)
        split, rest = split_point(center)
        for index, part in enumerate(pair_rows(split, rest, (2, 0, 1), False)):
            rows_ref[NUMER + index:NUMER + index + 1, :] = part
        for axis in range(3):
            rows_ref[KDIM + axis:KDIM + axis + 1, :] = center[axis]
        turned = rows_ref[...].T
        place = pl.ds(pl.multiple_of(turn * CHUNK, CHUNK), CHUNK)
        features = turned[:, 0:KDIM]
        lanes = lax.broadcasted_iota(jnp.int32, features.shape, 1)
        source_k_ref[place, :] = jnp.where(lanes < NUMER, features, 0.0).astype(BF16)
        source_d_ref[place, :] = jnp.where(lanes < NUMER, 0.0, features).astype(BF16)
        rest_place = pl.ds(pl.multiple_of(turn * (CHUNK - SQUARED), 8), CHUNK - SQUARED)
        for axis in range(3):
            source_b_ref[axis, rest_place, :] = jnp.broadcast_to(
                turned[SQUARED:, KDIM + axis:KDIM + axis + 1], (CHUNK - SQUARED, 128)
            )
        return carry

    lax.fori_loop(0, 2 * src_dev // CHUNK, source_chunk, 0, unroll=8)
    lax.fori_loop(0, row_total // 2, target_chunk, 0, unroll=8)


def kernel(
    padded, src_dev, row_total,
    sample_ref, conn_hbm, density_hbm, lattice_hbm, mode_hbm, pol_hbm, azi_hbm, azim_rows_hbm,
    polar_rows_hbm,
    out_ref,
    conn_ref, density_ref, lattice_ref, mode_ref, pol_ref, azi_ref, azim_rows_ref, polar_rows_ref,
    target_k_ref, target_c_ref, source_k_ref, source_d_ref, source_b_ref, table_ref, rows_ref,
    send_buf, recv_buf, load_sem, share_sem, send_sem, recv_sem,
):
    me = lax.axis_index("row")
    side = lax.rem(me, 2)
    sibling = me + 1 - 2 * side
    owners = row_total // 2
    own_half = pl.ds(pl.multiple_of(side * src_dev, src_dev), src_dev)
    loads = [
        pltpu.make_async_copy(source, place, load_sem.at[index])
        for index, (source, place) in enumerate((
            (conn_hbm, conn_ref), (density_hbm, density_ref.at[:, own_half]), (lattice_hbm, lattice_ref),
            (mode_hbm, mode_ref), (pol_hbm, pol_ref), (azi_hbm, azi_ref),
            (azim_rows_hbm, azim_rows_ref), (polar_rows_hbm, polar_rows_ref),
        ))
    ]
    for index in (3, 2, 5, 4, 6, 7, 0, 1):
        loads[index].start()
    peers = owners - 1

    def owner_of(turn):
        return 2 * lax.rem(me // 2 + 1 + turn, owners) + side

    barrier = pltpu.get_barrier_semaphore()
    pl.semaphore_signal(
        barrier, inc=1, device_id={"row": sibling}, device_id_type=pl.DeviceIdType.MESH
    )

    def greet(turn, carry):
        pl.semaphore_signal(
            barrier, inc=1, device_id={"row": owner_of(turn)}, device_id_type=pl.DeviceIdType.MESH
        )
        return carry

    lax.fori_loop(0, peers, greet, 0)
    share = pltpu.make_async_remote_copy(
        src_ref=density_ref.at[:, own_half],
        dst_ref=density_ref.at[:, own_half],
        send_sem=share_sem.at[0],
        recv_sem=share_sem.at[1],
        device_id={"row": sibling},
        device_id_type=pl.DeviceIdType.MESH,
    )

    def begin():
        loads[0].wait()
        loads[1].wait()
        pl.semaphore_wait(barrier, peers + 1)
        share.start()

    for load in loads[2:]:
        load.wait()
    geometry(
        padded, src_dev, row_total, begin,
        sample_ref, lattice_ref, mode_ref, conn_ref, pol_ref, azi_ref, azim_rows_ref,
        polar_rows_ref, target_k_ref, target_c_ref, source_k_ref, source_d_ref, source_b_ref,
        table_ref, rows_ref,
    )
    share.wait()

    def block(place_index, own):
        place = pl.ds(pl.multiple_of(place_index * BAND_DEV, BAND_DEV), BAND_DEV)
        target_k = target_k_ref[:, place]
        target = [target_c_ref[axis:axis + 1, place] for axis in range(3)]

        def products(first):
            if first >= 2 * src_dev:
                return None
            numer = jnp.dot(
                source_k_ref[first:first + SRC_TILE, :], target_k, preferred_element_type=F32
            )
            square = jnp.dot(
                source_d_ref[first:first + SQUARED, :], target_k, preferred_element_type=F32
            )
            return numer, square

        def weigh(first, tile):
            return jnp.dot(
                density_ref[:, first:first + SRC_TILE], tile, preferred_element_type=F32
            )

        def entries(first, numer, dist):
            if own and first // SRC_TILE * SRC_TILE % src_dev < BAND_DEV:
                same = (
                    lax.broadcasted_iota(jnp.int32, dist.shape, 0) + first
                    == lax.broadcasted_iota(jnp.int32, dist.shape, 1) + side * src_dev
                )
                inverse = lax.rsqrt(jnp.where(same, 1.0, dist))
                return jnp.where(same, 0.0, numer * inverse * (inverse * inverse)).astype(BF16)
            inverse = lax.rsqrt(dist)
            return (numer * inverse * (inverse * inverse)).astype(BF16)

        total = jnp.zeros((density_ref.shape[0], BAND_DEV), F32)
        current = products(0)
        before = None
        for first in range(0, 2 * src_dev, SRC_TILE):
            following = products(first + SRC_TILE)
            numer, square = current
            begin = first // SRC_TILE * (SRC_TILE - SQUARED)
            part = slice(begin, begin + SRC_TILE - SQUARED)
            dist = None
            for axis in range(3):
                wide = source_b_ref[axis, part, :]
                diff = target[axis] - jnp.concatenate([wide] * (BAND_DEV // 128), axis=1)
                dist = diff * diff if dist is None else dist + diff * diff
            tile = jnp.concatenate([
                entries(first, numer[:SQUARED], square),
                entries(first + SQUARED, numer[SQUARED:], dist),
            ], axis=0)
            if before is not None:
                total += weigh(first - SRC_TILE, before)
            before = tile
            current = following
        return total + weigh(2 * src_dev - SRC_TILE, before)

    def copy(turn):
        return pltpu.make_async_remote_copy(
            src_ref=send_buf.at[turn],
            dst_ref=recv_buf.at[turn],
            send_sem=send_sem.at[turn],
            recv_sem=recv_sem.at[turn],
            device_id={"row": owner_of(turn)},
            device_id_type=pl.DeviceIdType.MESH,
        )

    def step(turn, carry):
        send_buf[turn] = block(lax.rem(me // 2 + 1 + turn, owners), False).astype(BF16)
        copy(turn).start()
        return carry

    lax.fori_loop(0, peers, step, 0)
    local = density_ref[:, pl.ds(pl.multiple_of(side * src_dev, src_dev), BAND_DEV)]
    out_ref[...] = block(me // 2, True) + 0.5 * local.astype(F32)

    def collect(turn, carry):
        copy(turn).wait_recv()
        out_ref[...] += recv_buf[turn].astype(F32)
        return carry

    lax.fori_loop(0, peers, collect, 0)

    def finish(turn, carry):
        copy(turn).wait_send()
        return carry

    lax.fori_loop(0, peers, finish, 0)


def per_device(sample_index, lattice_vector, mode_table, connectivity, density):
    columns, src_dev = density.shape
    row_total = lax.axis_size("row")
    panel_total = src_dev * row_total
    cycle_count = panel_total // (2 * NPH) + 1
    padded = round_up(cycle_count, 16)
    band = BAND_DEV * row_total
    pol, azi, azim_rows, polar_rows = [jnp.asarray(t) for t in tables(cycle_count, padded)]
    vmem = pl.BlockSpec(memory_space=pltpu.VMEM)
    smem = pl.BlockSpec(memory_space=pltpu.SMEM)
    hbm = pl.BlockSpec(memory_space=pltpu.HBM)
    loaded = [
        connectivity, density, lattice_vector.reshape(1, -1), mode_table,
        pol, azi, azim_rows, polar_rows,
    ]
    sums = pl.pallas_call(
        functools.partial(kernel, padded, src_dev, row_total),
        out_shape=jax.ShapeDtypeStruct((columns, BAND_DEV), F32),
        in_specs=[smem] + [hbm] * len(loaded),
        out_specs=vmem,
        scratch_shapes=[
            pltpu.VMEM(connectivity.shape, jnp.int32),
            pltpu.VMEM((columns, 2 * src_dev), BF16),
        ] + [pltpu.VMEM(array.shape, array.dtype) for array in loaded[2:]] + [
            pltpu.VMEM((KDIM, band // 2), BF16),
            pltpu.VMEM((3, band // 2), F32),
            pltpu.VMEM((2 * src_dev, KDIM), BF16),
            pltpu.VMEM((2 * src_dev, KDIM), BF16),
            pltpu.VMEM((3, 2 * src_dev // SRC_TILE * (SRC_TILE - SQUARED), 128), F32),
            pltpu.VMEM((6 * padded + 16, NPH), BF16),
            pltpu.VMEM((KDIM + 8, CHUNK), F32),
            pltpu.VMEM((row_total // 2 - 1, columns, BAND_DEV), BF16),
            pltpu.VMEM((row_total // 2 - 1, columns, BAND_DEV), BF16),
            pltpu.SemaphoreType.DMA((len(loaded),)),
            pltpu.SemaphoreType.DMA((2,)),
            pltpu.SemaphoreType.DMA((row_total // 2 - 1,)),
            pltpu.SemaphoreType.DMA((row_total // 2 - 1,)),
        ],
        compiler_params=pltpu.CompilerParams(
            collective_id=0, has_side_effects=True, vmem_limit_bytes=63 << 20
        ),
        name="potential",
    )(sample_index, *loaded)
    return sums.T


def solution(mesh):
    placed = (P("sample"), P(), P(), P(), P(None, "row"))
    return jax.shard_map(
        per_device,
        mesh=mesh,
        in_specs=placed,
        out_specs=P(("sample", "row"), None),
        check_vma=False,
    )
```

```python
import functools
import math

import jax
import jax.numpy as jnp
import numpy as np
from jax import lax
from jax.experimental import pallas as pl
from jax.experimental.pallas import tpu as pltpu
from jax.sharding import PartitionSpec as P

NLAT = 32768
NPH = 256
LANES = 128
BAND_DEV = 256
POLAR = 32
AZIM = 32
AZIM_LOW = -16
NUMER = 32
SQUARE = 48
KDIM = NUMER + SQUARE
STAGED = KDIM + 8
SRC_TILE = 256
SQUARED = 176
PLAIN = SRC_TILE - SQUARED
ROW_STEP = 65

F32 = jnp.float32
BF16 = jnp.bfloat16


def round_up(value, step):
    return -(-value // step) * step


def split3(value):
    high = value.astype(BF16)
    rest = value - high.astype(F32)
    mid = rest.astype(BF16)
    low = (rest - mid.astype(F32)).astype(BF16)
    return high, mid, low


AXES = (2, 0, 1)


def pair_rows(split, rest):
    one = jnp.ones_like(rest)
    rows = []
    for axis in AXES:
        high = split[axis][0]
        whole = high * high
        first = whole.astype(BF16).astype(F32)
        rows += [one, first, -2.0 * high, one, whole - first]
    for part in split3(rest):
        rows += [one, part.astype(F32)]
    for axis in AXES:
        high, mid, low = [-2.0 * part for part in split[axis]]
        rows += [mid, high, mid, low, high, low, mid]
    return rows


def split_point(center):
    split = [[part.astype(F32) for part in split3(value)] for value in center]
    rest = None
    for value, parts in zip(center, split):
        term = (value - parts[0]) * (value + parts[0])
        rest = term if rest is None else rest + term
    return split, rest


def tables(cycle_count, padded):
    angle = np.pi * (np.arange(cycle_count) + 1.0) / (cycle_count + 1)
    azimuth = 2.0 * np.pi * np.arange(NPH) / NPH
    polar = np.arange(POLAR)
    azim = np.arange(AZIM) + AZIM_LOW
    pol = np.zeros((padded, 2 * POLAR), np.float32)
    pol[:cycle_count, :POLAR] = np.cos(angle[:, None] * polar[None])
    pol[:cycle_count, POLAR:] = np.sin(angle[:, None] * polar[None])
    azi = np.concatenate(
        [np.cos(azim[:, None] * azimuth[None]), -np.sin(azim[:, None] * azimuth[None])]
    ).astype(np.float32)
    blocks = -(-cycle_count // LANES)
    turn = np.zeros((round_up(2 + 2 * blocks, 8), LANES), np.float32)
    turn[0] = np.cos(azimuth[:LANES])
    turn[1] = np.sin(azimuth[:LANES])
    full = np.zeros((2, blocks * LANES))
    full[:, :cycle_count] = np.sin(angle), np.cos(angle)
    turn[2:2 + 2 * blocks] = full.reshape(2 * blocks, LANES)
    return pol, azi, turn


def dot_hi(left, right):
    return jnp.dot(left, right, precision=lax.Precision.HIGHEST, preferred_element_type=F32)


def radius_table(sample_ref, lattice_ref, mode_ref, pol_ref, azi_ref, radius_ref):
    steps = (sample_ref[0] * lattice_ref[...]) & (NLAT - 1)
    shifts = steps.astype(F32) / NLAT - 0.5
    polar = mode_ref[0:1, :]
    azim = mode_ref[1:2, :]
    scale = 1.0 + polar.astype(F32) + jnp.abs(azim.astype(F32))
    coef = 0.8 * shifts / (scale * scale)
    modes = coef.shape[1]
    at_polar = lax.broadcasted_iota(jnp.int32, (POLAR, modes), 0) == polar
    at_azim = lax.broadcasted_iota(jnp.int32, (AZIM, modes), 0) + AZIM_LOW == azim
    azim_hot = jnp.where(at_azim, 1.0, 0.0).astype(BF16)
    grid = jnp.zeros((POLAR, AZIM), F32)
    for part in split3(jnp.where(at_polar, coef, 0.0)):
        grid += lax.dot_general(part, azim_hot, (((1,), (1,)), ((), ())), preferred_element_type=F32)
    cos_half = dot_hi(grid, azi_ref[0:AZIM, :])
    sin_half = dot_hi(grid, azi_ref[AZIM:2 * AZIM, :])
    log_radius = dot_hi(pol_ref[:, 0:POLAR], cos_half) + dot_hi(pol_ref[:, POLAR:2 * POLAR], sin_half)
    radius = jnp.exp(log_radius)
    for half in range(NPH // LANES):
        radius_ref[half] = radius[:, LANES * half:LANES * half + LANES]


def corner_points(cycle_count, groups, conn_ref, turn_ref, radius_ref, corner_ref, vertex_ref, point_ref):
    for group in range(groups):
        corner_ref[8 * group:8 * group + 3, :] = conn_ref[:, LANES * group:LANES * group + LANES]
    for k in range(3):
        vertex_ref[k] = corner_ref[pl.ds(k, groups, stride=8), :]
    blocks = -(-cycle_count // LANES)
    halves = NPH // LANES
    step = min(cycle_count, ROW_STEP)
    whole = cycle_count // step

    def pick(table, row, lanes):
        wide = jnp.broadcast_to(table[pl.ds(row, 1), :], (groups, LANES))
        return jnp.take_along_axis(wide, lanes, axis=1)

    def corner(k, carry):
        vertex = vertex_ref[k]
        lane = vertex & (LANES - 1)
        line = vertex // LANES

        def pick_rows(row, count, found):
            found = list(found)
            for index in range(count):
                for half in range(halves):
                    here = line == halves * (row + index) + half
                    found[half] = jnp.where(here, pick(radius_ref.at[half], row + index, lane), found[half])
            return tuple(found)

        found = (jnp.zeros((groups, LANES), F32),) * halves
        if whole == 1:
            found = pick_rows(0, step, found)
        else:
            found = lax.fori_loop(0, whole, lambda turn, part: pick_rows(turn * step, step, part), found)
        found = pick_rows(whole * step, cycle_count - whole * step, found)
        radius = sum(found)
        cos_f = pick(turn_ref, 0, lane)
        sin_f = pick(turn_ref, 1, lane)
        cycle = line // halves
        cycle_lane = cycle & (LANES - 1)
        sin_t = pick(turn_ref, 2, cycle_lane)
        cos_t = pick(turn_ref, 2 + blocks, cycle_lane)
        for block in range(1, blocks):
            here = cycle // LANES == block
            sin_t = jnp.where(here, pick(turn_ref, 2 + block, cycle_lane), sin_t)
            cos_t = jnp.where(here, pick(turn_ref, 2 + blocks + block, cycle_lane), cos_t)
        ring = radius * sin_t
        ring = jnp.where(line % halves == 1, -ring, ring)
        point_ref[3 * k] = ring * cos_f
        point_ref[3 * k + 1] = ring * sin_f
        point_ref[3 * k + 2] = radius * cos_t
        return carry

    lax.fori_loop(0, 3, corner, 0)


def panel_geometry(point_ref, panel_ref):
    points = [[point_ref[3 * k + axis] for axis in range(3)] for k in range(3)]
    one = [points[1][axis] - points[0][axis] for axis in range(3)]
    two = [points[2][axis] - points[0][axis] for axis in range(3)]
    factor = 0.5 / (4.0 * math.pi)
    area = [
        factor * (one[1] * two[2] - one[2] * two[1]),
        factor * (one[2] * two[0] - one[0] * two[2]),
        factor * (one[0] * two[1] - one[1] * two[0]),
    ]
    for axis in range(3):
        panel_ref[0, axis] = (points[0][axis] + points[1][axis] + points[2][axis]) / 3.0
        panel_ref[0, 3 + axis] = area[axis]


def source_rows(center, area):
    rows = []
    for axis in range(3):
        high, mid, low = [part.astype(F32) for part in split3(area[axis])]
        rows += [high, mid, low, high, mid, high]
    base = -(center[0] * area[0] + center[1] * area[1] + center[2] * area[2])
    rows += [part.astype(F32) for part in split3(base)]
    rows += [None] * (NUMER - len(rows))
    split, rest = split_point(center)
    rows += pair_rows(split, rest)
    rows += [None] * (KDIM - len(rows))
    return rows + list(center)


def sources(src_dev, half, panel_ref, stage_ref, source_ref, source_b_ref):
    groups = src_dev // LANES
    center = [panel_ref[half, axis] for axis in range(3)]
    area = [panel_ref[half, 3 + axis] for axis in range(3)]
    for index, row in enumerate(source_rows(center, area)):
        if row is not None:
            stage_ref[pl.ds(index, groups, stride=STAGED), :] = row

    def turn_over(turn, carry):
        for step in range(SRC_TILE // LANES):
            place = pl.ds(pl.multiple_of((turn * (SRC_TILE // LANES) + step) * STAGED, 8), STAGED)
            turned = stage_ref[place, :].T
            start = pl.multiple_of(half * src_dev + turn * SRC_TILE + step * LANES, LANES)
            source_ref[pl.ds(start, LANES), :] = turned[:, 0:KDIM].astype(BF16)
            skip = max(SQUARED - step * LANES, 0)
            if skip < LANES:
                start = pl.multiple_of((half * (src_dev // SRC_TILE) + turn) * PLAIN, 8)
                for axis in range(3):
                    source_b_ref[axis, pl.ds(start, PLAIN), :] = jnp.broadcast_to(
                        turned[skip:, KDIM + axis:KDIM + axis + 1], (PLAIN, LANES)
                    )
        return carry

    lax.fori_loop(0, src_dev // SRC_TILE, turn_over, 0, unroll=4)


ONE_ROWS = [18, 19, 20] + [
    NUMER + index for index in (1, 4, 6, 9, 11, 14, 16, 18, 20)
]


def target_rows(center):
    high, mid, low = [part.astype(F32) for part in split3(center)]
    whole = high * high
    first = whole.astype(BF16).astype(F32)
    second = whole - first
    term = (center - high) * (center + high)
    rest = term[0:1] + term[1:2] + term[2:3]
    rows = {}
    for axis in range(3):
        h, m, l = [part[axis:axis + 1] for part in (high, mid, low)]
        for index, row in enumerate((h, h, h, m, m, l)):
            rows[6 * axis + index] = row
        place = AXES.index(axis)
        begin = NUMER + 5 * place
        rows[begin], rows[begin + 2], rows[begin + 3] = first[axis:axis + 1], h, second[axis:axis + 1]
        for index, row in enumerate((h, m, m, h, l, m, l)):
            rows[NUMER + 21 + 7 * place + index] = row
    for index, part in enumerate(split3(rest)):
        rows[NUMER + 15 + 2 * index] = part.astype(F32)
    return rows


def kernel(
    cycle_count, src_dev, row_total,
    sample_ref, conn_hbm, density_hbm, lattice_hbm, mode_hbm, pol_hbm, azi_hbm, turn_hbm,
    out_ref,
    conn_ref, density_ref, lattice_ref, mode_ref, pol_ref, azi_ref, turn_ref,
    radius_ref, corner_ref, vertex_ref, point_ref, panel_ref, stage_ref, band_ref, center_ref,
    source_ref, source_b_ref, send_buf, recv_buf, load_sem, share_sem, panel_sem, spread_sem, arrive_sem, send_sem, recv_sem,
):
    me = lax.axis_index("row")
    own = me // 2
    side = me % 2
    sibling = me + 1 - 2 * side
    owners = row_total // 2
    peers = owners - 1
    near = pl.ds(0, src_dev)
    far = pl.ds(src_dev, src_dev)
    loads = [
        pltpu.make_async_copy(source, place, load_sem.at[index])
        for index, (source, place) in enumerate((
            (mode_hbm, mode_ref), (lattice_hbm, lattice_ref), (azi_hbm, azi_ref), (pol_hbm, pol_ref),
            (conn_hbm.at[:, pl.ds(pl.multiple_of(me * src_dev, src_dev), src_dev)], conn_ref),
            (turn_hbm, turn_ref), (density_hbm, density_ref.at[:, near]),
        ))
    ]
    for load in loads:
        load.start()

    def owner_of(turn):
        return (own + 1 + turn) % owners

    def device_of(owner):
        return {"row": 2 * owner + side}

    barrier = pltpu.get_barrier_semaphore()
    pl.semaphore_signal(
        barrier, inc=1, device_id={"row": sibling}, device_id_type=pl.DeviceIdType.MESH
    )

    def greet(turn, carry):
        pl.semaphore_signal(
            barrier, inc=1, device_id=device_of(owner_of(turn)), device_id_type=pl.DeviceIdType.MESH
        )
        return carry

    lax.fori_loop(0, peers, greet, 0)
    share = pltpu.make_async_remote_copy(
        src_ref=density_ref.at[:, near],
        dst_ref=density_ref.at[:, far],
        send_sem=share_sem.at[0],
        recv_sem=share_sem.at[1],
        device_id={"row": sibling},
        device_id_type=pl.DeviceIdType.MESH,
    )

    swap = pltpu.make_async_remote_copy(
        src_ref=panel_ref.at[0],
        dst_ref=panel_ref.at[1],
        send_sem=panel_sem.at[0],
        recv_sem=panel_sem.at[1],
        device_id={"row": sibling},
        device_id_type=pl.DeviceIdType.MESH,
    )

    def spread(turn):
        return pltpu.make_async_remote_copy(
            src_ref=center_ref.at[own],
            dst_ref=center_ref.at[own],
            send_sem=spread_sem.at[turn],
            recv_sem=arrive_sem.at[own],
            device_id=device_of(owner_of(turn)),
            device_id_type=pl.DeviceIdType.MESH,
        )

    def arrive(owner):
        return pltpu.make_async_remote_copy(
            src_ref=center_ref.at[owner],
            dst_ref=center_ref.at[owner],
            send_sem=spread_sem.at[0],
            recv_sem=arrive_sem.at[owner],
            device_id=device_of(owner),
            device_id_type=pl.DeviceIdType.MESH,
        )

    def copy(turn):
        return pltpu.make_async_remote_copy(
            src_ref=send_buf.at[turn],
            dst_ref=recv_buf.at[turn],
            send_sem=send_sem.at[turn],
            recv_sem=recv_sem.at[turn],
            device_id=device_of(owner_of(turn)),
            device_id_type=pl.DeviceIdType.MESH,
        )

    for load in loads[:4]:
        load.wait()
    radius_table(sample_ref, lattice_ref, mode_ref, pol_ref, azi_ref, radius_ref)
    for load in loads[4:6]:
        load.wait()
    corner_points(
        cycle_count, src_dev // LANES, conn_ref, turn_ref, radius_ref, corner_ref, vertex_ref, point_ref
    )
    panel_geometry(point_ref, panel_ref)
    for axis in range(3):
        for group in range(BAND_DEV // LANES):
            center_ref[own, axis:axis + 1, LANES * group:LANES * group + LANES] = panel_ref[
                0, axis, group:group + 1, :
            ]
    center_ref[own, 3:4, :] = jnp.zeros((1, BAND_DEV), F32)
    pl.semaphore_wait(barrier, peers + 1)
    swap.start()

    def begin(turn, carry):
        spread(turn).start()
        return carry

    lax.fori_loop(0, peers, begin, 0)
    loads[6].wait()
    share.start()
    stage_ref[...] = jnp.zeros_like(stage_ref)
    sources(src_dev, 0, panel_ref, stage_ref, source_ref, source_b_ref)
    band_ref[...] = jnp.zeros_like(band_ref)
    for row in ONE_ROWS:
        band_ref[row:row + 1, :] = jnp.ones((1, BAND_DEV), F32)

    def block(owner, low, high, mine):
        center = center_ref[owner]
        target = [center[axis:axis + 1] for axis in range(3)]
        for index, row in target_rows(center).items():
            band_ref[index:index + 1, :] = row
        numer_k = band_ref[0:NUMER, :].astype(BF16)
        square_k = band_ref[NUMER:KDIM, :].astype(BF16)
        numer_k = jnp.concatenate([numer_k, jnp.zeros((SQUARE, BAND_DEV), BF16)], axis=0)
        square_k = jnp.concatenate([jnp.zeros((NUMER, BAND_DEV), BF16), square_k], axis=0)

        def products(first):
            if first >= high:
                return None
            numer = jnp.dot(
                source_ref[first:first + SRC_TILE, :], numer_k, preferred_element_type=F32
            )
            square = jnp.dot(
                source_ref[first:first + SQUARED, :], square_k, preferred_element_type=F32
            )
            return numer, square

        def weigh(first, tile):
            return jnp.dot(
                density_ref[:, first:first + SRC_TILE], tile, preferred_element_type=F32
            )

        def entries(first, numer, dist):
            if mine and first < BAND_DEV:
                same = (
                    lax.broadcasted_iota(jnp.int32, dist.shape, 0) + first
                    == lax.broadcasted_iota(jnp.int32, dist.shape, 1)
                )
                inverse = lax.rsqrt(jnp.where(same, 1.0, dist))
                return jnp.where(same, 0.0, numer * inverse * (inverse * inverse)).astype(BF16)
            inverse = lax.rsqrt(dist)
            return (numer * inverse * (inverse * inverse)).astype(BF16)

        total = jnp.zeros((density_ref.shape[0], BAND_DEV), F32)
        current = products(low)
        before = None
        for first in range(low, high, SRC_TILE):
            following = products(first + SRC_TILE)
            numer, square = current
            start = first // SRC_TILE * PLAIN
            dist = None
            for axis in range(3):
                wide = source_b_ref[axis, start:start + PLAIN, :]
                diff = target[axis] - jnp.concatenate([wide] * (BAND_DEV // LANES), axis=1)
                dist = diff * diff if dist is None else dist + diff * diff
            tile = jnp.concatenate([
                entries(first, numer[:SQUARED], square),
                entries(first + SQUARED, numer[SQUARED:], dist),
            ], axis=0)
            if before is not None:
                total += weigh(first - SRC_TILE, before)
            before = tile
            current = following
        return total + weigh(high - SRC_TILE, before)

    out_ref[...] = block(own, 0, src_dev, True) + 0.5 * density_ref[:, 0:BAND_DEV].astype(F32)
    swap.wait()
    sources(src_dev, 1, panel_ref, stage_ref, source_ref, source_b_ref)
    share.wait()

    def step(turn, carry):
        owner = owner_of(turn)
        arrive(owner).wait_recv()
        send_buf[turn] = block(owner, 0, 2 * src_dev, False).astype(BF16)
        copy(turn).start()
        return carry

    lax.fori_loop(0, peers, step, 0)
    out_ref[...] += block(own, src_dev, 2 * src_dev, False)

    def collect(turn, carry):
        copy(turn).wait_recv()
        out_ref[...] += recv_buf[turn].astype(F32)
        return carry

    lax.fori_loop(0, peers, collect, 0)

    def finish(turn, carry):
        copy(turn).wait_send()
        spread(turn).wait_send()
        return carry

    lax.fori_loop(0, peers, finish, 0)


def per_device(sample_index, lattice_vector, mode_table, connectivity, density):
    columns, src_dev = density.shape
    row_total = lax.axis_size("row")
    owners = row_total // 2
    cycle_count = src_dev * row_total // (2 * NPH) + 1
    padded = round_up(cycle_count, 16)
    pol, azi, turn = [jnp.asarray(t) for t in tables(cycle_count, padded)]
    groups = src_dev // LANES
    vmem = pl.BlockSpec(memory_space=pltpu.VMEM)
    smem = pl.BlockSpec(memory_space=pltpu.SMEM)
    hbm = pl.BlockSpec(memory_space=pltpu.HBM)
    small = [lattice_vector.reshape(1, -1), mode_table, pol, azi, turn]
    sums = pl.pallas_call(
        functools.partial(kernel, cycle_count, src_dev, row_total),
        out_shape=jax.ShapeDtypeStruct((columns, BAND_DEV), F32),
        in_specs=[smem] + [hbm] * (2 + len(small)),
        out_specs=vmem,
        scratch_shapes=[
            pltpu.VMEM((3, src_dev), jnp.int32),
            pltpu.VMEM((columns, 2 * src_dev), BF16),
        ] + [pltpu.VMEM(array.shape, array.dtype) for array in small] + [
            pltpu.VMEM((NPH // LANES, padded, LANES), F32),
            pltpu.VMEM((8 * groups, LANES), jnp.int32),
            pltpu.VMEM((3, groups, LANES), jnp.int32),
            pltpu.VMEM((9, groups, LANES), F32),
            pltpu.VMEM((2, 6, groups, LANES), F32),
            pltpu.VMEM((groups * STAGED, LANES), F32),
            pltpu.VMEM((KDIM, BAND_DEV), F32),
            pltpu.VMEM((owners, 4, BAND_DEV), F32),
            pltpu.VMEM((2 * src_dev, KDIM), BF16),
            pltpu.VMEM((3, 2 * src_dev // SRC_TILE * PLAIN, LANES), F32),
            pltpu.VMEM((owners - 1, columns, BAND_DEV), BF16),
            pltpu.VMEM((owners - 1, columns, BAND_DEV), BF16),
            pltpu.SemaphoreType.DMA((7,)),
            pltpu.SemaphoreType.DMA((2,)),
            pltpu.SemaphoreType.DMA((2,)),
            pltpu.SemaphoreType.DMA((owners - 1,)),
            pltpu.SemaphoreType.DMA((owners,)),
            pltpu.SemaphoreType.DMA((owners - 1,)),
            pltpu.SemaphoreType.DMA((owners - 1,)),
        ],
        compiler_params=pltpu.CompilerParams(
            collective_id=0, has_side_effects=True, vmem_limit_bytes=63 << 20
        ),
        name="potential",
    )(sample_index, connectivity, density, *small)
    return sums.T


def solution(mesh):
    placed = (P("sample"), P(), P(), P(), P(None, "row"))
    return jax.shard_map(
        per_device,
        mesh=mesh,
        in_specs=placed,
        out_specs=P(("sample", "row"), None),
        check_vma=False,
    )
```

```python
import functools
import math

import jax
import jax.numpy as jnp
import numpy as np
from jax import lax
from jax.experimental import pallas as pl
from jax.experimental.pallas import tpu as pltpu
from jax.sharding import PartitionSpec as P

NLAT = 32768
NPH = 256
LANES = 128
BAND_DEV = 256
POLAR = 32
AZIM = 32
AZIM_LOW = -16
NUMER = 32
SQUARE = 48
KDIM = NUMER + SQUARE
STAGED = KDIM + 8
SRC_TILE = 256
SQUARED = 176
PLAIN = SRC_TILE - SQUARED
ROW_STEP = 65

F32 = jnp.float32
BF16 = jnp.bfloat16


def round_up(value, step):
    return -(-value // step) * step


def split3(value):
    high = value.astype(BF16)
    rest = value - high.astype(F32)
    mid = rest.astype(BF16)
    low = (rest - mid.astype(F32)).astype(BF16)
    return high, mid, low


AXES = (2, 0, 1)


def pair_rows(split, rest):
    one = jnp.ones_like(rest)
    rows = []
    for axis in AXES:
        high = split[axis][0]
        whole = high * high
        first = whole.astype(BF16).astype(F32)
        rows += [one, first, -2.0 * high, one, whole - first]
    for part in split3(rest):
        rows += [one, part.astype(F32)]
    for axis in AXES:
        high, mid, low = [-2.0 * part for part in split[axis]]
        rows += [mid, high, mid, low, high, low, mid]
    return rows


def split_point(center):
    split = [[part.astype(F32) for part in split3(value)] for value in center]
    rest = None
    for value, parts in zip(center, split):
        term = (value - parts[0]) * (value + parts[0])
        rest = term if rest is None else rest + term
    return split, rest


def tables(cycle_count, padded):
    angle = np.pi * (np.arange(cycle_count) + 1.0) / (cycle_count + 1)
    azimuth = 2.0 * np.pi * np.arange(NPH) / NPH
    polar = np.arange(POLAR)
    azim = np.arange(AZIM) + AZIM_LOW
    pol = np.zeros((padded, 2 * POLAR), np.float32)
    pol[:cycle_count, :POLAR] = np.cos(angle[:, None] * polar[None])
    pol[:cycle_count, POLAR:] = np.sin(angle[:, None] * polar[None])
    azi = np.concatenate(
        [np.cos(azim[:, None] * azimuth[None]), -np.sin(azim[:, None] * azimuth[None])]
    ).astype(np.float32)
    blocks = -(-cycle_count // LANES)
    turn = np.zeros((round_up(2 + 2 * blocks, 8), LANES), np.float32)
    turn[0] = np.cos(azimuth[:LANES])
    turn[1] = np.sin(azimuth[:LANES])
    full = np.zeros((2, blocks * LANES))
    full[:, :cycle_count] = np.sin(angle), np.cos(angle)
    turn[2:2 + 2 * blocks] = full.reshape(2 * blocks, LANES)
    return pol, azi, turn


def dot_hi(left, right):
    return jnp.dot(left, right, precision=lax.Precision.HIGHEST, preferred_element_type=F32)


def radius_table(sample_ref, lattice_ref, mode_ref, pol_ref, azi_ref, radius_ref):
    steps = (sample_ref[0] * lattice_ref[...]) & (NLAT - 1)
    shifts = steps.astype(F32) / NLAT - 0.5
    polar = mode_ref[0:1, :]
    azim = mode_ref[1:2, :]
    scale = 1.0 + polar.astype(F32) + jnp.abs(azim.astype(F32))
    coef = 0.8 * shifts / (scale * scale)
    modes = coef.shape[1]
    at_polar = lax.broadcasted_iota(jnp.int32, (POLAR, modes), 0) == polar
    at_azim = lax.broadcasted_iota(jnp.int32, (AZIM, modes), 0) + AZIM_LOW == azim
    azim_hot = jnp.where(at_azim, 1.0, 0.0).astype(BF16)
    grid = jnp.zeros((POLAR, AZIM), F32)
    for part in split3(jnp.where(at_polar, coef, 0.0)):
        grid += lax.dot_general(part, azim_hot, (((1,), (1,)), ((), ())), preferred_element_type=F32)
    cos_half = dot_hi(grid, azi_ref[0:AZIM, :])
    sin_half = dot_hi(grid, azi_ref[AZIM:2 * AZIM, :])
    log_radius = dot_hi(pol_ref[:, 0:POLAR], cos_half) + dot_hi(pol_ref[:, POLAR:2 * POLAR], sin_half)
    radius = jnp.exp(log_radius)
    for half in range(NPH // LANES):
        radius_ref[half] = radius[:, LANES * half:LANES * half + LANES]


def corner_points(cycle_count, first, groups, conn_ref, turn_ref, radius_ref, corner_ref, vertex_ref, point_ref):
    for group in range(groups):
        corner_ref[8 * group:8 * group + 3, :] = conn_ref[
            :, first + LANES * group:first + LANES * group + LANES
        ]
    for k in range(3):
        vertex_ref[k] = corner_ref[pl.ds(k, groups, stride=8), :]
    blocks = -(-cycle_count // LANES)
    halves = NPH // LANES
    step = min(cycle_count, ROW_STEP)
    whole = cycle_count // step

    def pick(table, row, lanes):
        wide = jnp.broadcast_to(table[pl.ds(row, 1), :], (groups, LANES))
        return jnp.take_along_axis(wide, lanes, axis=1)

    def corner(k, carry):
        vertex = vertex_ref[k]
        lane = vertex & (LANES - 1)
        line = vertex // LANES

        def pick_rows(row, count, found):
            found = list(found)
            for index in range(count):
                for half in range(halves):
                    here = line == halves * (row + index) + half
                    found[half] = jnp.where(here, pick(radius_ref.at[half], row + index, lane), found[half])
            return tuple(found)

        found = (jnp.zeros((groups, LANES), F32),) * halves
        if whole == 1:
            found = pick_rows(0, step, found)
        else:
            found = lax.fori_loop(0, whole, lambda turn, part: pick_rows(turn * step, step, part), found)
        found = pick_rows(whole * step, cycle_count - whole * step, found)
        radius = sum(found)
        cos_f = pick(turn_ref, 0, lane)
        sin_f = pick(turn_ref, 1, lane)
        cycle = line // halves
        cycle_lane = cycle & (LANES - 1)
        sin_t = pick(turn_ref, 2, cycle_lane)
        cos_t = pick(turn_ref, 2 + blocks, cycle_lane)
        for block in range(1, blocks):
            here = cycle // LANES == block
            sin_t = jnp.where(here, pick(turn_ref, 2 + block, cycle_lane), sin_t)
            cos_t = jnp.where(here, pick(turn_ref, 2 + blocks + block, cycle_lane), cos_t)
        ring = radius * sin_t
        ring = jnp.where(line % halves == 1, -ring, ring)
        point_ref[3 * k] = ring * cos_f
        point_ref[3 * k + 1] = ring * sin_f
        point_ref[3 * k + 2] = radius * cos_t
        return carry

    lax.fori_loop(0, 3, corner, 0)


def panel_centers(point_ref):
    return [(point_ref[axis] + point_ref[3 + axis] + point_ref[6 + axis]) / 3.0 for axis in range(3)]


def panel_geometry(half, point_ref, panel_ref):
    points = [[point_ref[3 * k + axis] for axis in range(3)] for k in range(3)]
    one = [points[1][axis] - points[0][axis] for axis in range(3)]
    two = [points[2][axis] - points[0][axis] for axis in range(3)]
    factor = 0.5 / (4.0 * math.pi)
    area = [
        factor * (one[1] * two[2] - one[2] * two[1]),
        factor * (one[2] * two[0] - one[0] * two[2]),
        factor * (one[0] * two[1] - one[1] * two[0]),
    ]
    for axis, center in enumerate(panel_centers(point_ref)):
        panel_ref[half, axis] = center
        panel_ref[half, 3 + axis] = area[axis]


def source_rows(center, area):
    rows = []
    for axis in range(3):
        high, mid, low = [part.astype(F32) for part in split3(area[axis])]
        rows += [high, mid, low, high, mid, high]
    base = -(center[0] * area[0] + center[1] * area[1] + center[2] * area[2])
    rows += [part.astype(F32) for part in split3(base)]
    rows += [None] * (NUMER - len(rows))
    split, rest = split_point(center)
    rows += pair_rows(split, rest)
    rows += [None] * (KDIM - len(rows))
    return rows + list(center)


def sources(src_dev, half, panel_ref, stage_ref, source_ref, source_b_ref):
    groups = src_dev // LANES
    center = [panel_ref[half, axis] for axis in range(3)]
    area = [panel_ref[half, 3 + axis] for axis in range(3)]
    for index, row in enumerate(source_rows(center, area)):
        if row is not None:
            stage_ref[pl.ds(index, groups, stride=STAGED), :] = row

    def turn_over(turn, carry):
        for step in range(SRC_TILE // LANES):
            place = pl.ds(pl.multiple_of((turn * (SRC_TILE // LANES) + step) * STAGED, 8), STAGED)
            turned = stage_ref[place, :].T
            start = pl.multiple_of(half * src_dev + turn * SRC_TILE + step * LANES, LANES)
            source_ref[pl.ds(start, LANES), :] = turned[:, 0:KDIM].astype(BF16)
            skip = max(SQUARED - step * LANES, 0)
            if skip < LANES:
                start = pl.multiple_of((half * (src_dev // SRC_TILE) + turn) * PLAIN, 8)
                for axis in range(3):
                    source_b_ref[axis, pl.ds(start, PLAIN), :] = jnp.broadcast_to(
                        turned[skip:, KDIM + axis:KDIM + axis + 1], (PLAIN, LANES)
                    )
        return carry

    lax.fori_loop(0, src_dev // SRC_TILE, turn_over, 0, unroll=4)


ONE_ROWS = [18, 19, 20] + [
    NUMER + index for index in (1, 4, 6, 9, 11, 14, 16, 18, 20)
]


def target_rows(center):
    high, mid, low = [part.astype(F32) for part in split3(center)]
    whole = high * high
    first = whole.astype(BF16).astype(F32)
    second = whole - first
    term = (center - high) * (center + high)
    rest = term[0:1] + term[1:2] + term[2:3]
    rows = {}
    for axis in range(3):
        h, m, l = [part[axis:axis + 1] for part in (high, mid, low)]
        for index, row in enumerate((h, h, h, m, m, l)):
            rows[6 * axis + index] = row
        place = AXES.index(axis)
        begin = NUMER + 5 * place
        rows[begin], rows[begin + 2], rows[begin + 3] = first[axis:axis + 1], h, second[axis:axis + 1]
        for index, row in enumerate((h, m, m, h, l, m, l)):
            rows[NUMER + 21 + 7 * place + index] = row
    for index, part in enumerate(split3(rest)):
        rows[NUMER + 15 + 2 * index] = part.astype(F32)
    return rows


def kernel(
    cycle_count, src_dev, row_total,
    sample_ref, conn_hbm, density_hbm, lattice_hbm, mode_hbm, pol_hbm, azi_hbm, turn_hbm,
    out_ref,
    conn_ref, density_ref, lattice_ref, mode_ref, pol_ref, azi_ref, turn_ref,
    radius_ref, corner_ref, vertex_ref, point_ref, panel_ref, stage_ref, band_ref, center_ref,
    source_ref, source_b_ref, send_buf, recv_buf, load_sem, share_sem, send_sem, recv_sem,
):
    me = lax.axis_index("row")
    own = me // 2
    side = me % 2
    sibling = me + 1 - 2 * side
    owners = row_total // 2
    peers = owners - 1
    near = pl.ds(0, src_dev)
    far = pl.ds(src_dev, src_dev)
    loads = [
        pltpu.make_async_copy(source, place, load_sem.at[index])
        for index, (source, place) in enumerate((
            (mode_hbm, mode_ref), (lattice_hbm, lattice_ref), (azi_hbm, azi_ref), (pol_hbm, pol_ref),
            (conn_hbm.at[:, pl.ds(pl.multiple_of(me * src_dev, src_dev), src_dev)], conn_ref.at[:, near]),
            (turn_hbm, turn_ref),
            (conn_hbm.at[:, pl.ds(pl.multiple_of(sibling * src_dev, src_dev), src_dev)], conn_ref.at[:, far]),
            (density_hbm, density_ref.at[:, near]),
        ))
    ]
    loads += [
        pltpu.make_async_copy(
            conn_hbm.at[:, pl.ds(pl.multiple_of((2 * owner + side) * src_dev, src_dev), BAND_DEV)],
            conn_ref.at[:, pl.ds(2 * src_dev + owner * BAND_DEV, BAND_DEV)],
            load_sem.at[8 + owner],
        )
        for owner in range(owners)
    ]
    for load in loads:
        load.start()

    def at_least(value, bound):
        return (value - bound + row_total) // row_total

    def ring(turn):
        return (own + 1 + turn) % owners

    def owner_of(turn):
        early, place = peers // 2, peers - own
        moved = at_least(place, early + 1) * at_least(own, 1)
        first = moved * at_least(turn, early) * at_least(early, turn)
        later = moved * at_least(turn, early + 1) * at_least(place, turn)
        return (1 - first) * ring(turn - later)

    def device_of(owner):
        return {"row": 2 * owner + side}

    barrier = pltpu.get_barrier_semaphore()
    pl.semaphore_signal(
        barrier, inc=1, device_id={"row": sibling}, device_id_type=pl.DeviceIdType.MESH
    )

    def greet(turn, carry):
        pl.semaphore_signal(
            barrier, inc=1, device_id=device_of(ring(turn)), device_id_type=pl.DeviceIdType.MESH
        )
        return carry

    lax.fori_loop(0, peers, greet, 0)
    share = pltpu.make_async_remote_copy(
        src_ref=density_ref.at[:, near],
        dst_ref=density_ref.at[:, far],
        send_sem=share_sem.at[0],
        recv_sem=share_sem.at[1],
        device_id={"row": sibling},
        device_id_type=pl.DeviceIdType.MESH,
    )

    def copy(turn):
        return pltpu.make_async_remote_copy(
            src_ref=send_buf.at[turn],
            dst_ref=recv_buf.at[own],
            send_sem=send_sem.at[turn],
            recv_sem=recv_sem.at[own],
            device_id=device_of(owner_of(turn)),
            device_id_type=pl.DeviceIdType.MESH,
        )

    def arrival(owner):
        return pltpu.make_async_remote_copy(
            src_ref=send_buf.at[0],
            dst_ref=recv_buf.at[owner],
            send_sem=send_sem.at[0],
            recv_sem=recv_sem.at[owner],
            device_id=device_of(owner),
            device_id_type=pl.DeviceIdType.MESH,
        )

    stage_ref[...] = jnp.zeros_like(stage_ref)
    band_ref[...] = jnp.zeros_like(band_ref)
    for row in ONE_ROWS:
        band_ref[row:row + 1, :] = jnp.ones((1, BAND_DEV), F32)
    for load in loads[:4] + loads[5:6]:
        load.wait()
    radius_table(sample_ref, lattice_ref, mode_ref, pol_ref, azi_ref, radius_ref)
    groups = src_dev // LANES
    band = BAND_DEV // LANES

    def points(first):
        corner_points(
            cycle_count, first, groups,
            conn_ref, turn_ref, radius_ref, corner_ref, vertex_ref, point_ref,
        )

    for half, load in enumerate((loads[4], loads[6])):
        load.wait()
        points(half * src_dev)
        panel_geometry(half, point_ref, panel_ref)
        sources(src_dev, half, panel_ref, stage_ref, source_ref, source_b_ref)
    loads[7].wait()
    pl.semaphore_wait(barrier, peers + 1)
    share.start()
    for load in loads[8:]:
        load.wait()
    for first in range(0, owners, groups // band):
        points(2 * src_dev + first * BAND_DEV)
        for axis, center in enumerate(panel_centers(point_ref)):
            for group in range(groups):
                lanes = slice(LANES * (group % band), LANES * (group % band) + LANES)
                center_ref[first + group // band, axis:axis + 1, lanes] = center[group:group + 1]
    def block(owner, low, high, mine):
        center = center_ref[owner, 0:3, :]
        target = [center[axis:axis + 1] for axis in range(3)]
        for index, row in target_rows(center).items():
            band_ref[index:index + 1, :] = row
        numer_k = band_ref[0:NUMER, :].astype(BF16)
        square_k = band_ref[NUMER:KDIM, :].astype(BF16)
        numer_k = jnp.concatenate([numer_k, jnp.zeros((SQUARE, BAND_DEV), BF16)], axis=0)
        square_k = jnp.concatenate([jnp.zeros((NUMER, BAND_DEV), BF16), square_k], axis=0)

        def products(first):
            if first >= high:
                return None
            numer = jnp.dot(
                source_ref[first:first + SRC_TILE, :], numer_k, preferred_element_type=F32
            )
            square = jnp.dot(
                source_ref[first:first + SQUARED, :], square_k, preferred_element_type=F32
            )
            return numer, square

        def weigh(first, tile):
            return jnp.dot(
                density_ref[:, first:first + SRC_TILE], tile, preferred_element_type=F32
            )

        def entries(first, numer, dist):
            if mine and first < BAND_DEV:
                same = (
                    lax.broadcasted_iota(jnp.int32, dist.shape, 0) + first
                    == lax.broadcasted_iota(jnp.int32, dist.shape, 1)
                )
                inverse = lax.rsqrt(jnp.where(same, 1.0, dist))
                return jnp.where(same, 0.0, numer * inverse * (inverse * inverse)).astype(BF16)
            inverse = lax.rsqrt(dist)
            return (numer * inverse * (inverse * inverse)).astype(BF16)

        total = jnp.zeros((density_ref.shape[0], BAND_DEV), F32)
        current = products(low)
        before = None
        for first in range(low, high, SRC_TILE):
            following = products(first + SRC_TILE)
            numer, square = current
            start = first // SRC_TILE * PLAIN
            dist = None
            for axis in range(3):
                wide = source_b_ref[axis, start:start + PLAIN, :]
                diff = target[axis] - jnp.concatenate([wide] * (BAND_DEV // LANES), axis=1)
                dist = diff * diff if dist is None else dist + diff * diff
            tile = jnp.concatenate([
                entries(first, numer[:SQUARED], square),
                entries(first + SQUARED, numer[SQUARED:], dist),
            ], axis=0)
            if before is not None:
                total += weigh(first - SRC_TILE, before)
            before = tile
            current = following
        return total + weigh(high - SRC_TILE, before)

    out_ref[...] = block(own, 0, src_dev, True) + 0.5 * density_ref[:, 0:BAND_DEV].astype(F32)
    share.wait()

    def step(turn, carry):
        owner = owner_of(turn)
        send_buf[turn] = block(owner, 0, 2 * src_dev, False).astype(BF16)
        copy(turn).start()
        return carry

    lax.fori_loop(0, peers, step, 0)
    out_ref[...] += block(own, src_dev, 2 * src_dev, False)

    def collect(turn, carry):
        owner = ring(turn)
        arrival(owner).wait_recv()
        out_ref[...] += recv_buf[owner].astype(F32)
        return carry

    lax.fori_loop(0, peers, collect, 0)

    def finish(turn, carry):
        copy(turn).wait_send()
        return carry

    lax.fori_loop(0, peers, finish, 0)


def per_device(sample_index, lattice_vector, mode_table, connectivity, density):
    columns, src_dev = density.shape
    row_total = lax.axis_size("row")
    owners = row_total // 2
    cycle_count = src_dev * row_total // (2 * NPH) + 1
    padded = round_up(cycle_count, 16)
    pol, azi, turn = [jnp.asarray(t) for t in tables(cycle_count, padded)]
    groups = src_dev // LANES
    vmem = pl.BlockSpec(memory_space=pltpu.VMEM)
    smem = pl.BlockSpec(memory_space=pltpu.SMEM)
    hbm = pl.BlockSpec(memory_space=pltpu.HBM)
    small = [lattice_vector.reshape(1, -1), mode_table, pol, azi, turn]
    sums = pl.pallas_call(
        functools.partial(kernel, cycle_count, src_dev, row_total),
        out_shape=jax.ShapeDtypeStruct((columns, BAND_DEV), F32),
        in_specs=[smem] + [hbm] * (2 + len(small)),
        out_specs=vmem,
        scratch_shapes=[
            pltpu.VMEM((3, 2 * src_dev + owners * BAND_DEV), jnp.int32),
            pltpu.VMEM((columns, 2 * src_dev), BF16),
        ] + [pltpu.VMEM(array.shape, array.dtype) for array in small] + [
            pltpu.VMEM((NPH // LANES, padded, LANES), F32),
            pltpu.VMEM((8 * groups, LANES), jnp.int32),
            pltpu.VMEM((3, groups, LANES), jnp.int32),
            pltpu.VMEM((9, groups, LANES), F32),
            pltpu.VMEM((2, 6, groups, LANES), F32),
            pltpu.VMEM((groups * STAGED, LANES), F32),
            pltpu.VMEM((KDIM, BAND_DEV), F32),
            pltpu.VMEM((owners, 4, BAND_DEV), F32),
            pltpu.VMEM((2 * src_dev, KDIM), BF16),
            pltpu.VMEM((3, 2 * src_dev // SRC_TILE * PLAIN, LANES), F32),
            pltpu.VMEM((owners - 1, columns, BAND_DEV), BF16),
            pltpu.VMEM((owners, columns, BAND_DEV), BF16),
            pltpu.SemaphoreType.DMA((8 + owners,)),
            pltpu.SemaphoreType.DMA((2,)),
            pltpu.SemaphoreType.DMA((owners - 1,)),
            pltpu.SemaphoreType.DMA((owners,)),
        ],
        compiler_params=pltpu.CompilerParams(
            collective_id=0, has_side_effects=True, vmem_limit_bytes=32 << 20
        ),
        name="potential",
    )(sample_index, *[
        pltpu.with_memory_space_constraint(array, pltpu.HBM) for array in (connectivity, density, *small)
    ])
    return sums.T


def solution(mesh):
    placed = (P("sample"), P(), P(), P(), P(None, "row"))
    return jax.shard_map(
        per_device,
        mesh=mesh,
        in_specs=placed,
        out_specs=P(("sample", "row"), None),
        check_vma=False,
    )
```

```python
import functools
import math

import jax
import jax.numpy as jnp
import numpy as np
from jax import lax
from jax.experimental import pallas as pl
from jax.experimental.pallas import tpu as pltpu
from jax.sharding import PartitionSpec as P

NLAT = 32768
NPH = 256
LANES = 128
BAND_DEV = 256
POLAR = 32
AZIM = 32
AZIM_LOW = -16
NUMER = 32
SQUARE = 48
KDIM = NUMER + SQUARE
STAGED = KDIM + 8
SRC_TILE = 256
SQUARED = 176
PLAIN = SRC_TILE - SQUARED
ROW_STEP = 65

F32 = jnp.float32
BF16 = jnp.bfloat16


def round_up(value, step):
    return -(-value // step) * step


def split3(value):
    high = value.astype(BF16)
    rest = value - high.astype(F32)
    mid = rest.astype(BF16)
    low = (rest - mid.astype(F32)).astype(BF16)
    return high, mid, low


AXES = (2, 0, 1)


def pair_rows(split, rest):
    one = jnp.ones_like(rest)
    rows = []
    for axis in AXES:
        high = split[axis][0]
        whole = high * high
        first = whole.astype(BF16).astype(F32)
        rows += [one, first, -2.0 * high, one, whole - first]
    for part in split3(rest):
        rows += [one, part.astype(F32)]
    for axis in AXES:
        high, mid, low = [-2.0 * part for part in split[axis]]
        rows += [mid, high, mid, low, high, low, mid]
    return rows


def split_point(center):
    split = [[part.astype(F32) for part in split3(value)] for value in center]
    rest = None
    for value, parts in zip(center, split):
        term = (value - parts[0]) * (value + parts[0])
        rest = term if rest is None else rest + term
    return split, rest


def tables(cycle_count, padded):
    angle = np.pi * (np.arange(cycle_count) + 1.0) / (cycle_count + 1)
    azimuth = 2.0 * np.pi * np.arange(NPH) / NPH
    polar = np.arange(POLAR)
    azim = np.arange(AZIM) + AZIM_LOW
    pol = np.zeros((padded, 2 * POLAR), np.float32)
    pol[:cycle_count, :POLAR] = np.cos(angle[:, None] * polar[None])
    pol[:cycle_count, POLAR:] = np.sin(angle[:, None] * polar[None])
    azi = np.concatenate(
        [np.cos(azim[:, None] * azimuth[None]), -np.sin(azim[:, None] * azimuth[None])]
    ).astype(np.float32)
    upper = cycle_count - 1
    blocks = -(-upper // LANES)
    turn = np.zeros((round_up(2 + 4 * blocks, 8), LANES), np.float32)
    turn[0] = np.cos(azimuth[:LANES])
    turn[1] = np.sin(azimuth[:LANES])
    full = np.zeros((4, blocks * LANES))
    full[:, :upper] = np.sin(angle[:-1]), np.cos(angle[:-1]), np.sin(angle[1:]), np.cos(angle[1:])
    turn[2:2 + 4 * blocks] = full.reshape(4 * blocks, LANES)
    return pol, azi, turn


def dot_hi(left, right):
    return jnp.dot(left, right, precision=lax.Precision.HIGHEST, preferred_element_type=F32)


def radius_table(sample_ref, lattice_ref, mode_ref, pol_ref, azi_ref, radius_ref):
    steps = (sample_ref[0] * lattice_ref[...]) & (NLAT - 1)
    shifts = steps.astype(F32) / NLAT - 0.5
    polar = mode_ref[0:1, :]
    azim = mode_ref[1:2, :]
    scale = 1.0 + polar.astype(F32) + jnp.abs(azim.astype(F32))
    coef = 0.8 * shifts / (scale * scale)
    modes = coef.shape[1]
    at_polar = lax.broadcasted_iota(jnp.int32, (POLAR, modes), 0) == polar
    at_azim = lax.broadcasted_iota(jnp.int32, (AZIM, modes), 0) + AZIM_LOW == azim
    azim_hot = jnp.where(at_azim, 1.0, 0.0).astype(BF16)
    grid = jnp.zeros((POLAR, AZIM), F32)
    for part in split3(jnp.where(at_polar, coef, 0.0)):
        grid += lax.dot_general(part, azim_hot, (((1,), (1,)), ((), ())), preferred_element_type=F32)
    cos_half = dot_hi(grid, azi_ref[0:AZIM, :])
    sin_half = dot_hi(grid, azi_ref[AZIM:2 * AZIM, :])
    log_radius = dot_hi(pol_ref[:, 0:POLAR], cos_half) + dot_hi(pol_ref[:, POLAR:2 * POLAR], sin_half)
    radius = jnp.exp(log_radius)
    for half in range(NPH // LANES):
        radius_ref[half] = radius[:, LANES * half:LANES * half + LANES]


def corner_points(
    cycle_count, first, groups, conn_ref, turn_ref, radius_ref, corner_ref, vertex_ref, side_ref, point_ref
):
    for group in range(groups):
        corner_ref[8 * group:8 * group + 3, :] = conn_ref[
            :, first + LANES * group:first + LANES * group + LANES
        ]
    vertex = [corner_ref[pl.ds(k, groups, stride=8), :] for k in range(3)]
    azim = [v & (NPH - 1) for v in vertex]
    cycle = [v // NPH for v in vertex]
    here = jnp.minimum(jnp.minimum(cycle[0], cycle[1]), cycle[2])
    low = jnp.minimum(jnp.minimum(azim[0], azim[1]), azim[2])
    high = jnp.maximum(jnp.maximum(azim[0], azim[1]), azim[2])
    near = jnp.where(high - low > 1, high, low)
    halves = NPH // LANES
    for side, place in enumerate((near, (near + 1) & (NPH - 1))):
        vertex_ref[side] = place & (LANES - 1)
        vertex_ref[2 + side] = here * halves + place // LANES
    blocks = -(-(cycle_count - 1) // LANES)
    step = min(cycle_count, ROW_STEP)
    whole = cycle_count // step

    def pick(table, row, lanes):
        wide = jnp.broadcast_to(table[pl.ds(row, 1), :], (groups, LANES))
        return jnp.take_along_axis(wide, lanes, axis=1)

    def one_side(side, carry):
        lane = vertex_ref[side]
        line = vertex_ref[2 + side]

        def pick_rows(row, count, found):
            found = list(found)
            for index in range(count):
                for half in range(halves):
                    value = pick(radius_ref.at[half], row + index, lane)
                    for down in range(2):
                        match = line == halves * (row + index - down) + half
                        found[2 * half + down] = jnp.where(match, value, found[2 * half + down])
            return tuple(found)

        found = (jnp.zeros((groups, LANES), F32),) * (2 * halves)
        if whole == 1:
            found = pick_rows(0, step, found)
        else:
            found = lax.fori_loop(0, whole, lambda turn, part: pick_rows(turn * step, step, part), found)
        found = pick_rows(whole * step, cycle_count - whole * step, found)
        back = line % halves == 1
        side_ref[4 * side] = sum(found[0::2])
        side_ref[4 * side + 1] = sum(found[1::2])
        for index in range(2):
            value = pick(turn_ref, index, lane)
            side_ref[4 * side + 2 + index] = jnp.where(back, -value, value)
        return carry

    lax.fori_loop(0, 2, one_side, 0)
    lane = here & (LANES - 1)
    polar = []
    for index in range(4):
        value = pick(turn_ref, 2 + index * blocks, lane)
        for block in range(1, blocks):
            value = jnp.where(here // LANES == block, pick(turn_ref, 2 + index * blocks + block, lane), value)
        polar.append(value)
    cell = []
    for down in range(2):
        for side in range(2):
            radius, cos_f, sin_f = [side_ref[4 * side + index] for index in (down, 2, 3)]
            ring = radius * polar[2 * down]
            cell.append((ring * cos_f, ring * sin_f, radius * polar[2 * down + 1]))
    for k in range(3):
        down = cycle[k] != here
        far = azim[k] != near
        for axis in range(3):
            point_ref[3 * k + axis] = jnp.where(
                down,
                jnp.where(far, cell[3][axis], cell[2][axis]),
                jnp.where(far, cell[1][axis], cell[0][axis]),
            )


def panel_centers(point_ref):
    return [(point_ref[axis] + point_ref[3 + axis] + point_ref[6 + axis]) / 3.0 for axis in range(3)]


def panel_geometry(half, point_ref, panel_ref):
    points = [[point_ref[3 * k + axis] for axis in range(3)] for k in range(3)]
    one = [points[1][axis] - points[0][axis] for axis in range(3)]
    two = [points[2][axis] - points[0][axis] for axis in range(3)]
    factor = 0.5 / (4.0 * math.pi)
    area = [
        factor * (one[1] * two[2] - one[2] * two[1]),
        factor * (one[2] * two[0] - one[0] * two[2]),
        factor * (one[0] * two[1] - one[1] * two[0]),
    ]
    for axis, center in enumerate(panel_centers(point_ref)):
        panel_ref[half, axis] = center
        panel_ref[half, 3 + axis] = area[axis]


def source_rows(center, area):
    rows = []
    for axis in range(3):
        high, mid, low = [part.astype(F32) for part in split3(area[axis])]
        rows += [high, mid, low, high, mid, high]
    base = -(center[0] * area[0] + center[1] * area[1] + center[2] * area[2])
    rows += [part.astype(F32) for part in split3(base)]
    rows += [None] * (NUMER - len(rows))
    split, rest = split_point(center)
    rows += pair_rows(split, rest)
    rows += [None] * (KDIM - len(rows))
    return rows + list(center)


def sources(src_dev, half, panel_ref, stage_ref, source_ref, source_b_ref):
    groups = src_dev // LANES
    center = [panel_ref[half, axis] for axis in range(3)]
    area = [panel_ref[half, 3 + axis] for axis in range(3)]
    for index, row in enumerate(source_rows(center, area)):
        if row is not None:
            stage_ref[pl.ds(index, groups, stride=STAGED), :] = row

    def turn_over(turn, carry):
        for step in range(SRC_TILE // LANES):
            place = pl.ds(pl.multiple_of((turn * (SRC_TILE // LANES) + step) * STAGED, 8), STAGED)
            turned = stage_ref[place, :].T
            start = pl.multiple_of(half * src_dev + turn * SRC_TILE + step * LANES, LANES)
            source_ref[pl.ds(start, LANES), :] = turned[:, 0:KDIM].astype(BF16)
            skip = max(SQUARED - step * LANES, 0)
            if skip < LANES:
                start = pl.multiple_of((half * (src_dev // SRC_TILE) + turn) * PLAIN, 8)
                for axis in range(3):
                    source_b_ref[axis, pl.ds(start, PLAIN), :] = jnp.broadcast_to(
                        turned[skip:, KDIM + axis:KDIM + axis + 1], (PLAIN, LANES)
                    )
        return carry

    lax.fori_loop(0, src_dev // SRC_TILE, turn_over, 0, unroll=4)


ONE_ROWS = [18, 19, 20] + [
    NUMER + index for index in (1, 4, 6, 9, 11, 14, 16, 18, 20)
]


def target_rows(center):
    high, mid, low = [part.astype(F32) for part in split3(center)]
    whole = high * high
    first = whole.astype(BF16).astype(F32)
    second = whole - first
    term = (center - high) * (center + high)
    rest = term[0:1] + term[1:2] + term[2:3]
    rows = {}
    for axis in range(3):
        h, m, l = [part[axis:axis + 1] for part in (high, mid, low)]
        for index, row in enumerate((h, h, h, m, m, l)):
            rows[6 * axis + index] = row
        place = AXES.index(axis)
        begin = NUMER + 5 * place
        rows[begin], rows[begin + 2], rows[begin + 3] = first[axis:axis + 1], h, second[axis:axis + 1]
        for index, row in enumerate((h, m, m, h, l, m, l)):
            rows[NUMER + 21 + 7 * place + index] = row
    for index, part in enumerate(split3(rest)):
        rows[NUMER + 15 + 2 * index] = part.astype(F32)
    return rows


def kernel(
    cycle_count, src_dev, row_total,
    sample_ref, conn_hbm, density_hbm, lattice_hbm, mode_hbm, pol_hbm, azi_hbm, turn_hbm,
    out_ref,
    conn_ref, density_ref, lattice_ref, mode_ref, pol_ref, azi_ref, turn_ref,
    radius_ref, corner_ref, vertex_ref, side_ref, point_ref, panel_ref, stage_ref, band_ref, center_ref,
    source_ref, source_b_ref, send_buf, recv_buf, load_sem, share_sem, send_sem, recv_sem,
):
    me = lax.axis_index("row")
    own = me // 2
    side = me % 2
    sibling = me + 1 - 2 * side
    owners = row_total // 2
    peers = owners - 1
    near = pl.ds(0, src_dev)
    far = pl.ds(src_dev, src_dev)
    loads = [
        pltpu.make_async_copy(source, place, load_sem.at[index])
        for index, (source, place) in enumerate((
            (mode_hbm, mode_ref), (lattice_hbm, lattice_ref), (azi_hbm, azi_ref), (pol_hbm, pol_ref),
            (conn_hbm.at[:, pl.ds(pl.multiple_of(me * src_dev, src_dev), src_dev)], conn_ref.at[:, near]),
            (turn_hbm, turn_ref),
            (conn_hbm.at[:, pl.ds(pl.multiple_of(sibling * src_dev, src_dev), src_dev)], conn_ref.at[:, far]),
            (density_hbm, density_ref.at[:, near]),
        ))
    ]
    loads += [
        pltpu.make_async_copy(
            conn_hbm.at[:, pl.ds(pl.multiple_of((2 * owner + side) * src_dev, src_dev), BAND_DEV)],
            conn_ref.at[:, pl.ds(2 * src_dev + owner * BAND_DEV, BAND_DEV)],
            load_sem.at[8 + owner],
        )
        for owner in range(owners)
    ]
    for load in loads:
        load.start()

    def at_least(value, bound):
        return (value - bound + row_total) // row_total

    def ring(turn):
        return (own + 1 + turn) % owners

    def owner_of(turn):
        early, place = peers // 2, peers - own
        moved = at_least(place, early + 1) * at_least(own, 1)
        first = moved * at_least(turn, early) * at_least(early, turn)
        later = moved * at_least(turn, early + 1) * at_least(place, turn)
        return (1 - first) * ring(turn - later)

    def device_of(owner):
        return {"row": 2 * owner + side}

    barrier = pltpu.get_barrier_semaphore()
    pl.semaphore_signal(
        barrier, inc=1, device_id={"row": sibling}, device_id_type=pl.DeviceIdType.MESH
    )

    def greet(turn, carry):
        pl.semaphore_signal(
            barrier, inc=1, device_id=device_of(ring(turn)), device_id_type=pl.DeviceIdType.MESH
        )
        return carry

    lax.fori_loop(0, peers, greet, 0)
    share = pltpu.make_async_remote_copy(
        src_ref=density_ref.at[:, near],
        dst_ref=density_ref.at[:, far],
        send_sem=share_sem.at[0],
        recv_sem=share_sem.at[1],
        device_id={"row": sibling},
        device_id_type=pl.DeviceIdType.MESH,
    )

    def copy(turn):
        return pltpu.make_async_remote_copy(
            src_ref=send_buf.at[turn],
            dst_ref=recv_buf.at[own],
            send_sem=send_sem.at[turn],
            recv_sem=recv_sem.at[own],
            device_id=device_of(owner_of(turn)),
            device_id_type=pl.DeviceIdType.MESH,
        )

    def arrival(owner):
        return pltpu.make_async_remote_copy(
            src_ref=send_buf.at[0],
            dst_ref=recv_buf.at[owner],
            send_sem=send_sem.at[0],
            recv_sem=recv_sem.at[owner],
            device_id=device_of(owner),
            device_id_type=pl.DeviceIdType.MESH,
        )

    stage_ref[...] = jnp.zeros_like(stage_ref)
    band_ref[...] = jnp.zeros_like(band_ref)
    for row in ONE_ROWS:
        band_ref[row:row + 1, :] = jnp.ones((1, BAND_DEV), F32)
    for load in loads[:4] + loads[5:6]:
        load.wait()
    radius_table(sample_ref, lattice_ref, mode_ref, pol_ref, azi_ref, radius_ref)
    groups = src_dev // LANES
    band = BAND_DEV // LANES

    def points(first):
        corner_points(
            cycle_count, first, groups,
            conn_ref, turn_ref, radius_ref, corner_ref, vertex_ref, side_ref, point_ref,
        )

    for half, load in enumerate((loads[4], loads[6])):
        load.wait()
        points(half * src_dev)
        panel_geometry(half, point_ref, panel_ref)
        sources(src_dev, half, panel_ref, stage_ref, source_ref, source_b_ref)
    loads[7].wait()
    pl.semaphore_wait(barrier, peers + 1)
    share.start()
    for load in loads[8:]:
        load.wait()
    for first in range(0, owners, groups // band):
        points(2 * src_dev + first * BAND_DEV)
        for axis, center in enumerate(panel_centers(point_ref)):
            for group in range(groups):
                lanes = slice(LANES * (group % band), LANES * (group % band) + LANES)
                center_ref[first + group // band, axis:axis + 1, lanes] = center[group:group + 1]
    def block(owner, mine):
        center = center_ref[owner, 0:3, :]
        target = [center[axis:axis + 1] for axis in range(3)]
        for index, row in target_rows(center).items():
            band_ref[index:index + 1, :] = row
        numer_k = band_ref[0:NUMER, :].astype(BF16)
        square_k = band_ref[NUMER:KDIM, :].astype(BF16)
        numer_k = jnp.concatenate([numer_k, jnp.zeros((SQUARE, BAND_DEV), BF16)], axis=0)
        square_k = jnp.concatenate([jnp.zeros((NUMER, BAND_DEV), BF16), square_k], axis=0)

        def products(first):
            if first >= 2 * src_dev:
                return None
            numer = jnp.dot(
                source_ref[first:first + SRC_TILE, :], numer_k, preferred_element_type=F32
            )
            square = jnp.dot(
                source_ref[first:first + SQUARED, :], square_k, preferred_element_type=F32
            )
            return numer, square

        def weigh(first, tile):
            return jnp.dot(
                density_ref[:, first:first + SRC_TILE], tile, preferred_element_type=F32
            )

        def entries(first, numer, dist):
            if mine and first < BAND_DEV:
                same = (
                    lax.broadcasted_iota(jnp.int32, dist.shape, 0) + first
                    == lax.broadcasted_iota(jnp.int32, dist.shape, 1)
                )
                inverse = lax.rsqrt(jnp.where(same, 1.0, dist))
                return jnp.where(same, 0.0, numer * inverse * (inverse * inverse)).astype(BF16)
            inverse = lax.rsqrt(dist)
            return (numer * inverse * (inverse * inverse)).astype(BF16)

        total = jnp.zeros((density_ref.shape[0], BAND_DEV), F32)
        current = products(0)
        before = None
        for first in range(0, 2 * src_dev, SRC_TILE):
            following = products(first + SRC_TILE)
            numer, square = current
            start = first // SRC_TILE * PLAIN
            dist = None
            for axis in range(3):
                wide = source_b_ref[axis, start:start + PLAIN, :]
                diff = target[axis] - jnp.concatenate([wide] * (BAND_DEV // LANES), axis=1)
                dist = diff * diff if dist is None else dist + diff * diff
            tile = jnp.concatenate([
                entries(first, numer[:SQUARED], square),
                entries(first + SQUARED, numer[SQUARED:], dist),
            ], axis=0)
            if before is not None:
                total += weigh(first - SRC_TILE, before)
            before = tile
            current = following
        return total + weigh(2 * src_dev - SRC_TILE, before)

    share.wait()

    def step(turn, carry):
        owner = owner_of(turn)
        send_buf[turn] = block(owner, False).astype(BF16)
        copy(turn).start()
        return carry

    lax.fori_loop(0, peers, step, 0)
    out_ref[...] = block(own, True) + 0.5 * density_ref[:, 0:BAND_DEV].astype(F32)

    def collect(turn, carry):
        owner = ring(turn)
        arrival(owner).wait_recv()
        out_ref[...] += recv_buf[owner].astype(F32)
        return carry

    lax.fori_loop(0, peers, collect, 0)

    def finish(turn, carry):
        copy(turn).wait_send()
        return carry

    lax.fori_loop(0, peers, finish, 0)


def per_device(sample_index, lattice_vector, mode_table, connectivity, density):
    columns, src_dev = density.shape
    row_total = lax.axis_size("row")
    owners = row_total // 2
    cycle_count = src_dev * row_total // (2 * NPH) + 1
    padded = round_up(cycle_count, 16)
    pol, azi, turn = [jnp.asarray(t) for t in tables(cycle_count, padded)]
    groups = src_dev // LANES
    vmem = pl.BlockSpec(memory_space=pltpu.VMEM)
    smem = pl.BlockSpec(memory_space=pltpu.SMEM)
    hbm = pl.BlockSpec(memory_space=pltpu.HBM)
    small = [lattice_vector.reshape(1, -1), mode_table, pol, azi, turn]
    sums = pl.pallas_call(
        functools.partial(kernel, cycle_count, src_dev, row_total),
        out_shape=jax.ShapeDtypeStruct((columns, BAND_DEV), F32),
        in_specs=[smem] + [hbm] * (2 + len(small)),
        out_specs=vmem,
        scratch_shapes=[
            pltpu.VMEM((3, 2 * src_dev + owners * BAND_DEV), jnp.int32),
            pltpu.VMEM((columns, 2 * src_dev), BF16),
        ] + [pltpu.VMEM(array.shape, array.dtype) for array in small] + [
            pltpu.VMEM((NPH // LANES, padded, LANES), F32),
            pltpu.VMEM((8 * groups, LANES), jnp.int32),
            pltpu.VMEM((4, groups, LANES), jnp.int32),
            pltpu.VMEM((8, groups, LANES), F32),
            pltpu.VMEM((9, groups, LANES), F32),
            pltpu.VMEM((2, 6, groups, LANES), F32),
            pltpu.VMEM((groups * STAGED, LANES), F32),
            pltpu.VMEM((KDIM, BAND_DEV), F32),
            pltpu.VMEM((owners, 4, BAND_DEV), F32),
            pltpu.VMEM((2 * src_dev, KDIM), BF16),
            pltpu.VMEM((3, 2 * src_dev // SRC_TILE * PLAIN, LANES), F32),
            pltpu.VMEM((owners - 1, columns, BAND_DEV), BF16),
            pltpu.VMEM((owners, columns, BAND_DEV), BF16),
            pltpu.SemaphoreType.DMA((8 + owners,)),
            pltpu.SemaphoreType.DMA((2,)),
            pltpu.SemaphoreType.DMA((owners - 1,)),
            pltpu.SemaphoreType.DMA((owners,)),
        ],
        compiler_params=pltpu.CompilerParams(
            collective_id=0, has_side_effects=True, vmem_limit_bytes=32 << 20
        ),
        name="potential",
    )(sample_index, *[
        pltpu.with_memory_space_constraint(array, pltpu.HBM) for array in (connectivity, density, *small)
    ])
    return sums.T


def solution(mesh):
    placed = (P("sample"), P(), P(), P(), P(None, "row"))
    return jax.shard_map(
        per_device,
        mesh=mesh,
        in_specs=placed,
        out_specs=P(("sample", "row"), None),
        check_vma=False,
    )
```

```python
import functools
import math

import jax
import jax.numpy as jnp
import numpy as np
from jax import lax
from jax.experimental import pallas as pl
from jax.experimental.pallas import tpu as pltpu
from jax.sharding import PartitionSpec as P

NLAT = 32768
NPH = 256
LANES = 128
BAND_DEV = 256
POLAR = 32
AZIM = 32
AZIM_LOW = -16
NUMER = 32
SQUARE = 48
KDIM = NUMER + SQUARE
STAGED = KDIM + 8
SRC_TILE = 256
SQUARED = 176
PLAIN = SRC_TILE - SQUARED
ROW_STEP = 65

F32 = jnp.float32
BF16 = jnp.bfloat16


def round_up(value, step):
    return -(-value // step) * step


def split3(value):
    high = value.astype(BF16)
    rest = value - high.astype(F32)
    mid = rest.astype(BF16)
    low = (rest - mid.astype(F32)).astype(BF16)
    return high, mid, low


AXES = (2, 0, 1)


def pair_rows(split, rest):
    one = jnp.ones_like(rest)
    rows = []
    for axis in AXES:
        high = split[axis][0]
        whole = high * high
        first = whole.astype(BF16).astype(F32)
        rows += [one, first, -2.0 * high, one, whole - first]
    for part in split3(rest):
        rows += [one, part.astype(F32)]
    for axis in AXES:
        high, mid, low = [-2.0 * part for part in split[axis]]
        rows += [mid, high, mid, low, high, low, mid]
    return rows


def split_point(center):
    split = [[part.astype(F32) for part in split3(value)] for value in center]
    rest = None
    for value, parts in zip(center, split):
        term = (value - parts[0]) * (value + parts[0])
        rest = term if rest is None else rest + term
    return split, rest


def tables(cycle_count, padded):
    angle = np.pi * (np.arange(cycle_count) + 1.0) / (cycle_count + 1)
    azimuth = 2.0 * np.pi * np.arange(NPH) / NPH
    polar = np.arange(POLAR)
    azim = np.arange(AZIM) + AZIM_LOW
    pol = np.zeros((padded, 2 * POLAR), np.float32)
    pol[:cycle_count, :POLAR] = np.cos(angle[:, None] * polar[None])
    pol[:cycle_count, POLAR:] = np.sin(angle[:, None] * polar[None])
    azi = np.concatenate(
        [np.cos(azim[:, None] * azimuth[None]), -np.sin(azim[:, None] * azimuth[None])]
    ).astype(np.float32)
    upper = cycle_count - 1
    blocks = -(-upper // LANES)
    turn = np.zeros((round_up(2 + 4 * blocks, 8), LANES), np.float32)
    turn[0] = np.cos(azimuth[:LANES])
    turn[1] = np.sin(azimuth[:LANES])
    full = np.zeros((4, blocks * LANES))
    full[:, :upper] = np.sin(angle[:-1]), np.cos(angle[:-1]), np.sin(angle[1:]), np.cos(angle[1:])
    turn[2:2 + 4 * blocks] = full.reshape(4 * blocks, LANES)
    return pol, azi, turn


def dot_hi(left, right):
    return jnp.dot(left, right, precision=lax.Precision.HIGHEST, preferred_element_type=F32)


def radius_table(sample_ref, lattice_ref, mode_ref, pol_ref, azi_ref, radius_ref):
    steps = (sample_ref[0] * lattice_ref[...]) & (NLAT - 1)
    shifts = steps.astype(F32) / NLAT - 0.5
    polar = mode_ref[0:1, :]
    azim = mode_ref[1:2, :]
    scale = 1.0 + polar.astype(F32) + jnp.abs(azim.astype(F32))
    coef = 0.8 * shifts / (scale * scale)
    modes = coef.shape[1]
    at_polar = lax.broadcasted_iota(jnp.int32, (POLAR, modes), 0) == polar
    at_azim = lax.broadcasted_iota(jnp.int32, (AZIM, modes), 0) + AZIM_LOW == azim
    azim_hot = jnp.where(at_azim, 1.0, 0.0).astype(BF16)
    grid = jnp.zeros((POLAR, AZIM), F32)
    for part in split3(jnp.where(at_polar, coef, 0.0)):
        grid += lax.dot_general(part, azim_hot, (((1,), (1,)), ((), ())), preferred_element_type=F32)
    cos_half = dot_hi(grid, azi_ref[0:AZIM, :])
    sin_half = dot_hi(grid, azi_ref[AZIM:2 * AZIM, :])
    log_radius = dot_hi(pol_ref[:, 0:POLAR], cos_half) + dot_hi(pol_ref[:, POLAR:2 * POLAR], sin_half)
    radius = jnp.exp(log_radius)
    for half in range(NPH // LANES):
        radius_ref[half] = radius[:, LANES * half:LANES * half + LANES]


def corner_points(
    cycle_count, first, groups, conn_ref, turn_ref, radius_ref, corner_ref, vertex_ref, side_ref, point_ref
):
    for group in range(groups):
        corner_ref[8 * group:8 * group + 3, :] = conn_ref[
            :, first + LANES * group:first + LANES * group + LANES
        ]
    vertex = [corner_ref[pl.ds(k, groups, stride=8), :] for k in range(3)]
    azim = [v & (NPH - 1) for v in vertex]
    cycle = [v // NPH for v in vertex]
    here = jnp.minimum(jnp.minimum(cycle[0], cycle[1]), cycle[2])
    low = jnp.minimum(jnp.minimum(azim[0], azim[1]), azim[2])
    high = jnp.maximum(jnp.maximum(azim[0], azim[1]), azim[2])
    near = jnp.where(high - low > 1, high, low)
    halves = NPH // LANES
    for side, place in enumerate((near, (near + 1) & (NPH - 1))):
        vertex_ref[side] = place & (LANES - 1)
        vertex_ref[2 + side] = here * halves + place // LANES
    blocks = -(-(cycle_count - 1) // LANES)
    step = min(cycle_count, ROW_STEP)
    whole = cycle_count // step

    def pick(table, row, lanes):
        wide = jnp.broadcast_to(table[pl.ds(row, 1), :], (groups, LANES))
        return jnp.take_along_axis(wide, lanes, axis=1)

    def one_side(side, carry):
        lane = vertex_ref[side]
        line = vertex_ref[2 + side]

        def pick_rows(row, count, found):
            found = list(found)
            for index in range(count):
                for half in range(halves):
                    value = pick(radius_ref.at[half], row + index, lane)
                    for down in range(2):
                        match = line == halves * (row + index - down) + half
                        found[2 * half + down] = jnp.where(match, value, found[2 * half + down])
            return tuple(found)

        found = (jnp.zeros((groups, LANES), F32),) * (2 * halves)
        if whole == 1:
            found = pick_rows(0, step, found)
        else:
            found = lax.fori_loop(0, whole, lambda turn, part: pick_rows(turn * step, step, part), found)
        found = pick_rows(whole * step, cycle_count - whole * step, found)
        back = line % halves == 1
        side_ref[4 * side] = sum(found[0::2])
        side_ref[4 * side + 1] = sum(found[1::2])
        for index in range(2):
            value = pick(turn_ref, index, lane)
            side_ref[4 * side + 2 + index] = jnp.where(back, -value, value)
        return carry

    lax.fori_loop(0, 2, one_side, 0)
    lane = here & (LANES - 1)
    polar = []
    for index in range(4):
        value = pick(turn_ref, 2 + index * blocks, lane)
        for block in range(1, blocks):
            value = jnp.where(here // LANES == block, pick(turn_ref, 2 + index * blocks + block, lane), value)
        polar.append(value)
    cell = []
    for down in range(2):
        for side in range(2):
            radius, cos_f, sin_f = [side_ref[4 * side + index] for index in (down, 2, 3)]
            ring = radius * polar[2 * down]
            cell.append((ring * cos_f, ring * sin_f, radius * polar[2 * down + 1]))
    for k in range(3):
        down = cycle[k] != here
        far = azim[k] != near
        for axis in range(3):
            point_ref[3 * k + axis] = jnp.where(
                down,
                jnp.where(far, cell[3][axis], cell[2][axis]),
                jnp.where(far, cell[1][axis], cell[0][axis]),
            )


def panel_centers(point_ref):
    return [(point_ref[axis] + point_ref[3 + axis] + point_ref[6 + axis]) / 3.0 for axis in range(3)]


def panel_geometry(half, point_ref, panel_ref):
    points = [[point_ref[3 * k + axis] for axis in range(3)] for k in range(3)]
    one = [points[1][axis] - points[0][axis] for axis in range(3)]
    two = [points[2][axis] - points[0][axis] for axis in range(3)]
    factor = 0.5 / (4.0 * math.pi)
    area = [
        factor * (one[1] * two[2] - one[2] * two[1]),
        factor * (one[2] * two[0] - one[0] * two[2]),
        factor * (one[0] * two[1] - one[1] * two[0]),
    ]
    for axis, center in enumerate(panel_centers(point_ref)):
        panel_ref[half, axis] = center
        panel_ref[half, 3 + axis] = area[axis]


def source_rows(center, area):
    rows = []
    for axis in range(3):
        high, mid, low = [part.astype(F32) for part in split3(area[axis])]
        rows += [high, mid, low, high, mid, high]
    base = -(center[0] * area[0] + center[1] * area[1] + center[2] * area[2])
    rows += [part.astype(F32) for part in split3(base)]
    rows += [None] * (NUMER - len(rows))
    split, rest = split_point(center)
    rows += pair_rows(split, rest)
    rows += [None] * (KDIM - len(rows))
    return rows + list(center)


def sources(src_dev, half, panel_ref, stage_ref, source_ref, source_b_ref):
    groups = src_dev // LANES
    center = [panel_ref[half, axis] for axis in range(3)]
    area = [panel_ref[half, 3 + axis] for axis in range(3)]
    for index, row in enumerate(source_rows(center, area)):
        if row is not None:
            stage_ref[pl.ds(index, groups, stride=STAGED), :] = row

    def turn_over(turn, carry):
        for step in range(SRC_TILE // LANES):
            place = pl.ds(pl.multiple_of((turn * (SRC_TILE // LANES) + step) * STAGED, 8), STAGED)
            turned = stage_ref[place, :].T
            start = pl.multiple_of(half * src_dev + turn * SRC_TILE + step * LANES, LANES)
            source_ref[pl.ds(start, LANES), :] = turned[:, 0:KDIM].astype(BF16)
            skip = max(SQUARED - step * LANES, 0)
            if skip < LANES:
                start = pl.multiple_of((half * (src_dev // SRC_TILE) + turn) * PLAIN, 8)
                for axis in range(3):
                    source_b_ref[axis, pl.ds(start, PLAIN), :] = jnp.broadcast_to(
                        turned[skip:, KDIM + axis:KDIM + axis + 1], (PLAIN, LANES)
                    )
        return carry

    lax.fori_loop(0, src_dev // SRC_TILE, turn_over, 0, unroll=4)


ONE_ROWS = [18, 19, 20] + [
    NUMER + index for index in (1, 4, 6, 9, 11, 14, 16, 18, 20)
]


def target_rows(center):
    high, mid, low = [part.astype(F32) for part in split3(center)]
    whole = high * high
    first = whole.astype(BF16).astype(F32)
    second = whole - first
    term = (center - high) * (center + high)
    rest = term[0:1] + term[1:2] + term[2:3]
    rows = {}
    for axis in range(3):
        h, m, l = [part[axis:axis + 1] for part in (high, mid, low)]
        for index, row in enumerate((h, h, h, m, m, l)):
            rows[6 * axis + index] = row
        place = AXES.index(axis)
        begin = NUMER + 5 * place
        rows[begin], rows[begin + 2], rows[begin + 3] = first[axis:axis + 1], h, second[axis:axis + 1]
        for index, row in enumerate((h, m, m, h, l, m, l)):
            rows[NUMER + 21 + 7 * place + index] = row
    for index, part in enumerate(split3(rest)):
        rows[NUMER + 15 + 2 * index] = part.astype(F32)
    return rows


def kernel(
    cycle_count, src_dev, row_total,
    sample_ref, conn_hbm, density_hbm, lattice_hbm, mode_hbm, pol_hbm, azi_hbm, turn_hbm,
    out_ref,
    conn_ref, density_ref, lattice_ref, mode_ref, pol_ref, azi_ref, turn_ref,
    radius_ref, corner_ref, vertex_ref, side_ref, point_ref, panel_ref, stage_ref, band_ref, center_ref,
    source_ref, source_b_ref, send_buf, recv_buf, load_sem, share_sem, send_sem, recv_sem,
):
    me = lax.axis_index("row")
    own = me // 2
    side = me % 2
    sibling = me + 1 - 2 * side
    owners = row_total // 2
    peers = owners - 1
    near = pl.ds(0, src_dev)
    far = pl.ds(src_dev, src_dev)
    loads = [
        pltpu.make_async_copy(source, place, load_sem.at[index])
        for index, (source, place) in enumerate((
            (mode_hbm, mode_ref), (lattice_hbm, lattice_ref), (azi_hbm, azi_ref), (pol_hbm, pol_ref),
            (conn_hbm.at[:, pl.ds(pl.multiple_of(me * src_dev, src_dev), src_dev)], conn_ref.at[:, near]),
            (turn_hbm, turn_ref),
            (conn_hbm.at[:, pl.ds(pl.multiple_of(sibling * src_dev, src_dev), src_dev)], conn_ref.at[:, far]),
            (density_hbm, density_ref.at[:, near]),
        ))
    ]
    loads += [
        pltpu.make_async_copy(
            conn_hbm.at[:, pl.ds(pl.multiple_of((2 * owner + side) * src_dev, src_dev), BAND_DEV)],
            conn_ref.at[:, pl.ds(2 * src_dev + owner * BAND_DEV, BAND_DEV)],
            load_sem.at[8 + owner],
        )
        for owner in range(owners)
    ]
    for load in loads:
        load.start()

    def at_least(value, bound):
        return (value - bound + row_total) // row_total

    def ring(turn):
        return (own + 1 + turn) % owners

    def owner_of(turn):
        early, place = peers // 2, peers - own
        moved = at_least(place, early + 1) * at_least(own, 1)
        first = moved * at_least(turn, early) * at_least(early, turn)
        later = moved * at_least(turn, early + 1) * at_least(place, turn)
        return (1 - first) * ring(turn - later)

    def device_of(owner):
        return {"row": 2 * owner + side}

    barrier = pltpu.get_barrier_semaphore()
    pl.semaphore_signal(
        barrier, inc=1, device_id={"row": sibling}, device_id_type=pl.DeviceIdType.MESH
    )

    def greet(turn, carry):
        pl.semaphore_signal(
            barrier, inc=1, device_id=device_of(ring(turn)), device_id_type=pl.DeviceIdType.MESH
        )
        return carry

    lax.fori_loop(0, peers, greet, 0)
    share = pltpu.make_async_remote_copy(
        src_ref=density_ref.at[:, near],
        dst_ref=density_ref.at[:, far],
        send_sem=share_sem.at[0],
        recv_sem=share_sem.at[1],
        device_id={"row": sibling},
        device_id_type=pl.DeviceIdType.MESH,
    )

    def copy(turn):
        return pltpu.make_async_remote_copy(
            src_ref=send_buf.at[turn],
            dst_ref=recv_buf.at[own],
            send_sem=send_sem.at[turn],
            recv_sem=recv_sem.at[own],
            device_id=device_of(owner_of(turn)),
            device_id_type=pl.DeviceIdType.MESH,
        )

    def arrival(owner):
        return pltpu.make_async_remote_copy(
            src_ref=send_buf.at[0],
            dst_ref=recv_buf.at[owner],
            send_sem=send_sem.at[0],
            recv_sem=recv_sem.at[owner],
            device_id=device_of(owner),
            device_id_type=pl.DeviceIdType.MESH,
        )

    stage_ref[...] = jnp.zeros_like(stage_ref)
    band_ref[...] = jnp.zeros_like(band_ref)
    for row in ONE_ROWS:
        band_ref[row:row + 1, :] = jnp.ones((1, BAND_DEV), F32)
    for load in loads[:4] + loads[5:6]:
        load.wait()
    radius_table(sample_ref, lattice_ref, mode_ref, pol_ref, azi_ref, radius_ref)
    groups = src_dev // LANES
    band = BAND_DEV // LANES

    def points(first):
        corner_points(
            cycle_count, first, groups,
            conn_ref, turn_ref, radius_ref, corner_ref, vertex_ref, side_ref, point_ref,
        )

    for half, load in enumerate((loads[4], loads[6])):
        load.wait()
        points(half * src_dev)
        panel_geometry(half, point_ref, panel_ref)
        sources(src_dev, half, panel_ref, stage_ref, source_ref, source_b_ref)
    loads[7].wait()
    pl.semaphore_wait(barrier, peers + 1)
    share.start()
    for load in loads[8:]:
        load.wait()
    for first in range(0, owners, groups // band):
        points(2 * src_dev + first * BAND_DEV)
        for axis, center in enumerate(panel_centers(point_ref)):
            for group in range(groups):
                lanes = slice(LANES * (group % band), LANES * (group % band) + LANES)
                center_ref[first + group // band, axis:axis + 1, lanes] = center[group:group + 1]
    def block(owner, mine):
        center = center_ref[owner, 0:3, :]
        target = [center[axis:axis + 1] for axis in range(3)]
        for index, row in target_rows(center).items():
            band_ref[index:index + 1, :] = row
        numer_k = band_ref[0:NUMER, :].astype(BF16)
        square_k = band_ref[NUMER:KDIM, :].astype(BF16)
        numer_k = jnp.concatenate([numer_k, jnp.zeros((SQUARE, BAND_DEV), BF16)], axis=0)
        square_k = jnp.concatenate([jnp.zeros((NUMER, BAND_DEV), BF16), square_k], axis=0)

        def products(first):
            if first >= 2 * src_dev:
                return None
            numer = jnp.dot(
                source_ref[first:first + SRC_TILE, :], numer_k, preferred_element_type=F32
            )
            square = jnp.dot(
                source_ref[first:first + SQUARED, :], square_k, preferred_element_type=F32
            )
            return numer, square

        def weigh(first, tile):
            return jnp.dot(
                density_ref[:, first:first + SRC_TILE], tile, preferred_element_type=F32
            )

        def entries(first, numer, dist):
            if mine and first < BAND_DEV:
                same = (
                    lax.broadcasted_iota(jnp.int32, dist.shape, 0) + first
                    == lax.broadcasted_iota(jnp.int32, dist.shape, 1)
                )
                inverse = lax.rsqrt(jnp.where(same, 1.0, dist))
                return jnp.where(same, 0.0, numer * inverse * (inverse * inverse)).astype(BF16)
            inverse = lax.rsqrt(dist)
            return (numer * inverse * (inverse * inverse)).astype(BF16)

        total = jnp.zeros((density_ref.shape[0], BAND_DEV), F32)
        current = products(0)
        before = None
        for first in range(0, 2 * src_dev, SRC_TILE):
            following = products(first + SRC_TILE)
            numer, square = current
            start = first // SRC_TILE * PLAIN
            dist = None
            for axis in range(3):
                wide = source_b_ref[axis, start:start + PLAIN, :]
                diff = target[axis] - jnp.concatenate([wide] * (BAND_DEV // LANES), axis=1)
                dist = diff * diff if dist is None else dist + diff * diff
            tile = jnp.concatenate([
                entries(first, numer[:SQUARED], square),
                entries(first + SQUARED, numer[SQUARED:], dist),
            ], axis=0)
            if before is not None:
                total += weigh(first - SRC_TILE, before)
            before = tile
            current = following
        return total + weigh(2 * src_dev - SRC_TILE, before)

    share.wait()

    def step(turn, carry):
        owner = owner_of(turn)
        send_buf[turn] = block(owner, False).astype(BF16)
        copy(turn).start()
        return carry

    lax.fori_loop(0, peers, step, 0)
    out_ref[...] = block(own, True) + 0.5 * density_ref[:, 0:BAND_DEV].astype(F32)

    def collect(turn, carry):
        owner = ring(peers - 1 - turn)
        arrival(owner).wait_recv()
        out_ref[...] += recv_buf[owner].astype(F32)
        return carry

    lax.fori_loop(0, peers, collect, 0)

    def finish(turn, carry):
        copy(turn).wait_send()
        return carry

    lax.fori_loop(0, peers, finish, 0)


def per_device(sample_index, lattice_vector, mode_table, connectivity, density):
    columns, src_dev = density.shape
    row_total = lax.axis_size("row")
    owners = row_total // 2
    cycle_count = src_dev * row_total // (2 * NPH) + 1
    padded = round_up(cycle_count, 16)
    pol, azi, turn = [jnp.asarray(t) for t in tables(cycle_count, padded)]
    groups = src_dev // LANES
    vmem = pl.BlockSpec(memory_space=pltpu.VMEM)
    smem = pl.BlockSpec(memory_space=pltpu.SMEM)
    hbm = pl.BlockSpec(memory_space=pltpu.HBM)
    small = [lattice_vector.reshape(1, -1), mode_table, pol, azi, turn]
    sums = pl.pallas_call(
        functools.partial(kernel, cycle_count, src_dev, row_total),
        out_shape=jax.ShapeDtypeStruct((columns, BAND_DEV), F32),
        in_specs=[smem] + [hbm] * (2 + len(small)),
        out_specs=vmem,
        scratch_shapes=[
            pltpu.VMEM((3, 2 * src_dev + owners * BAND_DEV), jnp.int32),
            pltpu.VMEM((columns, 2 * src_dev), BF16),
        ] + [pltpu.VMEM(array.shape, array.dtype) for array in small] + [
            pltpu.VMEM((NPH // LANES, padded, LANES), F32),
            pltpu.VMEM((8 * groups, LANES), jnp.int32),
            pltpu.VMEM((4, groups, LANES), jnp.int32),
            pltpu.VMEM((8, groups, LANES), F32),
            pltpu.VMEM((9, groups, LANES), F32),
            pltpu.VMEM((2, 6, groups, LANES), F32),
            pltpu.VMEM((groups * STAGED, LANES), F32),
            pltpu.VMEM((KDIM, BAND_DEV), F32),
            pltpu.VMEM((owners, 4, BAND_DEV), F32),
            pltpu.VMEM((2 * src_dev, KDIM), BF16),
            pltpu.VMEM((3, 2 * src_dev // SRC_TILE * PLAIN, LANES), F32),
            pltpu.VMEM((owners - 1, columns, BAND_DEV), BF16),
            pltpu.VMEM((owners, columns, BAND_DEV), BF16),
            pltpu.SemaphoreType.DMA((8 + owners,)),
            pltpu.SemaphoreType.DMA((2,)),
            pltpu.SemaphoreType.DMA((owners - 1,)),
            pltpu.SemaphoreType.DMA((owners,)),
        ],
        compiler_params=pltpu.CompilerParams(
            collective_id=0, has_side_effects=True, vmem_limit_bytes=32 << 20
        ),
        name="potential",
    )(sample_index, *[
        pltpu.with_memory_space_constraint(array, pltpu.HBM) for array in (connectivity, density, *small)
    ])
    return sums.T


def solution(mesh):
    placed = (P("sample"), P(), P(), P(), P(None, "row"))
    return jax.shard_map(
        per_device,
        mesh=mesh,
        in_specs=placed,
        out_specs=P(("sample", "row"), None),
        check_vma=False,
    )
```
